256 devices in a mesh: slab: 64 (over z, y, core), dom: 4 (over x).
Axes of the slice: x: 4, y: 4, z: 8, core: 2. Of those that a mesh axis runs over, the one named last changes fastest.
Arguments:
- base_cells: int32 [3, 65536], P(None, ('slab', 'dom')), may hold values from 0 to 511, as said below
- offsets: float32 [3, 65536], P(None, ('slab', 'dom')), may hold values from 0 to 1
- charges: float32 [65536], P(('slab', 'dom')), may hold values from -4 to 4
- bias_coupling: float32 [65536], P(('slab', 'dom')), may hold values from -4 to 4
- counts: int32 [256], P(('slab', 'dom')), may hold values from 128 to 256, as said below
- green: float32 [256, 512, 256], P(None, 'slab', 'dom'), as said below
Outputs:
- potential: float32 [256, 512, 512], P('slab', 'dom')
- gradient: float32 [65536], P(('slab', 'dom'))
The draws below stay inside these ranges and needn't reach their ends.
Inputs may be any that keep to these rules, and one draw needn't show every extreme that they name: `base_cells`: an atom in slot a belongs to device a // 256, which is slab index (a // 256) // 4 and dom index (a // 256) % 4 of the mesh; its base cell has first coordinate in that slab's 4 planes, second coordinate in that dom index's 128 rows, third coordinate anywhere in 0..511. `counts`: A multiple of 128 of at least half of 256; equal to 256 on at least one device; a device's atoms fill its first slots. `green`: zero at the zero wavenumber and positive elsewhere.
All inputs are finite; a program needn't handle non-finite values.
Results may differ from the reference program's by a relative error of at most 0.000086.
Values sent between devices are 32-bit elements; how exact they have to be, the bound alone decides.
A program may use at most 64 MiB of HBM per device.

```python
import jax
import jax.numpy as jnp

XD = 4
NY = 512
NZ = 512
ATOM_DEV = 256
YD = 128
NX = 256
KH = 256
ATOMS = 65536
N_SLAB = 64
N_DOM = 4


def draw_base_cells(key, part):
    slot_index = jnp.arange(ATOMS, dtype=jnp.int32)
    owner = slot_index // ATOM_DEV
    slab_number = owner // N_DOM
    dom_number = owner % N_DOM
    key_x, key_y, key_z = jax.random.split(key, 3)
    cell_x = XD * slab_number + jax.random.randint(key_x, (ATOMS,), 0, XD)
    cell_y = YD * dom_number + jax.random.randint(key_y, (ATOMS,), 0, YD)
    cell_z = jax.random.randint(key_z, (ATOMS,), 0, NZ)
    return jnp.stack([cell_x, cell_y, cell_z]).astype(jnp.int32)


def draw_counts(key, part):
    total_devices = N_SLAB * N_DOM
    key_cut, key_full = jax.random.split(key)
    removed = jax.random.randint(key_cut, (total_devices,), 0, ATOM_DEV // 256 + 1)
    full_device = jax.random.randint(key_full, (), 0, total_devices)
    removed = jnp.where(jnp.arange(total_devices, dtype=jnp.int32) == full_device, 0, removed)
    return (ATOM_DEV - 128 * removed).astype(jnp.int32)


def draw_green(key, part):
    wave_x = jnp.arange(NX, dtype=jnp.int32)[:, None, None]
    wave_y = jnp.arange(NY, dtype=jnp.int32)[None, :, None]
    wave_z = jnp.arange(KH, dtype=jnp.int32)[None, None, :]
    sine_x = jnp.sin(jnp.pi * wave_x.astype(jnp.float32) / NX)
    sine_y = jnp.sin(jnp.pi * wave_y.astype(jnp.float32) / NY)
    sine_z = jnp.sin(jnp.pi * wave_z.astype(jnp.float32) / NZ)
    squared = 4.0 * (sine_x * sine_x + sine_y * sine_y + sine_z * sine_z)
    rough = jnp.exp(jax.random.uniform(key, (NX, NY, KH), jnp.float32, -0.693, 0.693))
    nonzero = wave_x + wave_y + wave_z > 0
    safe = jnp.where(nonzero, squared, 1.0)
    return jnp.where(nonzero, 8.0 * rough / safe, 0.0).astype(jnp.float32)


def steps_of(key, shape, pieces, low, top_value):
    loudness, own = 1.0, jax.random.fold_in(key, 6)
    for axis_at, parts in pieces:
        steps = jnp.exp(jax.random.uniform(jax.random.fold_in(own, axis_at), (parts,), jnp.float32, low / len(pieces), top_value / len(pieces)))
        loudness = loudness * jnp.repeat(steps, shape[axis_at] // parts).reshape([-1 if axis == axis_at else 1 for axis in range(len(shape))])
    return loudness


def centred(stream_key, shape, deviation, bound, cuts=(), kind=jnp.bfloat16):
    drawn = deviation * jax.random.normal(stream_key, shape, jnp.float32)
    if cuts:
        drawn = drawn * steps_of(stream_key, shape, cuts, -0.22, 0.18)
    return jnp.clip(drawn, -bound, bound).astype(kind)


def setup_inputs(seed: int = 0) -> dict:
    streams_of = jax.random.split(jax.random.key(seed), 7)
    base_cells = draw_base_cells(jax.random.fold_in(streams_of[6], 71), 0)
    offsets = jnp.clip(1.0 * jax.random.uniform(streams_of[1], (3, ATOMS), jnp.float32) ** steps_of(streams_of[1], (3, ATOMS), ((1, 256),), -0.2, 0.2), 0.0, 1.0)
    charges = centred(streams_of[2], (ATOMS,), 1.0, 4.0, ((0, 256),), jnp.float32)
    bias_coupling = centred(streams_of[3], (ATOMS,), 1.0, 4.0, ((0, 256),), jnp.float32)
    counts = draw_counts(jax.random.fold_in(streams_of[6], 71), 0)
    green = draw_green(jax.random.fold_in(streams_of[6], 71), 0)
    return {"base_cells": base_cells, "offsets": offsets, "charges": charges, "bias_coupling": bias_coupling, "counts": counts, "green": green}


def spline_rows(frac):
    inner = 1.0 - frac
    square = frac * frac
    cube = square * frac
    return jnp.stack([inner * inner * inner / 6.0, (3.0 * cube - 6.0 * square + 4.0) / 6.0, (-3.0 * cube + 3.0 * square + 3.0 * frac + 1.0) / 6.0, cube / 6.0])


def reference(base_cells, offsets, charges, bias_coupling, counts, green):
    slot_index = jnp.arange(ATOMS, dtype=jnp.int32)
    alive_mask = (slot_index % ATOM_DEV) < counts[slot_index // ATOM_DEV]
    weights = [spline_rows(offsets[axis_index]) for axis_index in range(3)]
    cell_list = []
    product_list = []
    for step_x in range(4):
        for step_y in range(4):
            for step_z in range(4):
                index_x = (base_cells[0] + step_x) % NX
                index_y = (base_cells[1] + step_y) % NY
                index_z = (base_cells[2] + step_z) % NZ
                cell_list.append(((index_x * NY + index_y) * NZ + index_z).astype(jnp.int32))
                product_list.append(weights[0][step_x] * weights[1][step_y] * weights[2][step_z])
    cell_index = jnp.stack(cell_list)
    products = jnp.stack(product_list)
    amounts = products * jnp.where(alive_mask, charges, 0.0)[None, :]
    flat_grid = jnp.zeros((NX * NY * NZ,), jnp.float32).at[cell_index.reshape(-1)].add(amounts.reshape(-1))
    spectrum = jnp.fft.rfftn(flat_grid.reshape(NX, NY, NZ))
    extended = jnp.concatenate([green, jnp.zeros((NX, NY, 1), jnp.float32)], 2)
    potential = jnp.fft.irfftn(spectrum * extended, s=(NX, NY, NZ)).astype(jnp.float32)
    sampled = jnp.sum(potential.reshape(-1)[cell_index] * products, 0)
    gradient = jnp.where(alive_mask, bias_coupling * sampled, 0.0)
    return potential, gradient
```

```python
import functools

import numpy as np
import jax
import jax.numpy as jnp
from jax import lax
from jax.experimental import pallas as pl
from jax.experimental.pallas import tpu as pltpu
from jax.sharding import PartitionSpec as P

XD = 4
NY = 512
NZ = 512
NX = 256
N_SLAB = 64
N_DOM = 4
ROWS = NY // N_DOM
KY = NY // N_SLAB
ATOMS = 256
C = 128
MESH = pl.DeviceIdType.MESH
F32 = jnp.float32
BF16 = jnp.bfloat16
EXTRA = 16


def halves(table):
    table = np.asarray(table, np.float32)
    high = table.astype(jnp.bfloat16)
    low = (table - high.astype(np.float32)).astype(jnp.bfloat16)
    return np.stack([high, low])


def constants():
    kz_local = NZ // 2 // N_DOM
    kz = np.arange(NZ // 2)
    angle = 2 * np.pi * ((kz[:, None] * np.arange(NZ)[None, :]) % NZ) / NZ
    fz = np.stack([np.cos(angle).reshape(N_DOM, kz_local, NZ), -np.sin(angle).reshape(N_DOM, kz_local, NZ)], 1)
    fz = fz.reshape(2 * kz_local * N_DOM, NZ)
    k = np.arange(256)
    even = 2 * np.pi * ((k[:, None] * k[None, :]) % 256) / 256
    odd = 2 * np.pi * ((k[:, None] * (2 * k[None, :] + 1)) % 512) / 512
    cs_even = np.concatenate([np.cos(even), np.sin(even)], 1)
    cs_odd = np.concatenate([np.cos(odd), np.sin(odd)], 1)
    t, s = np.arange(4)[:, None], np.arange(32)[None, :]
    back_even, back_odd = [], []
    for part in range(2):
        cols = (8 * s + 4 * part + t).reshape(-1)
        back_even.append(np.concatenate([np.cos(even)[:, cols], np.sin(even)[:, cols]], 1))
        back_odd.append(np.concatenate([np.cos(odd).T[:, cols], np.sin(odd).T[:, cols]], 1))
    return (
        halves(fz),
        halves(cs_even),
        halves(cs_odd),
        halves(np.stack(back_even)),
        halves(np.stack(back_odd)),
    )


def split(value):
    high = value.astype(BF16)
    low = (value - high.astype(F32)).astype(BF16)
    return high, low


NN = (((1,), (0,)), ((), ()))
NT = (((1,), (1,)), ((), ()))


def dot3(a, b, dims=NN):
    def dot(x, y):
        return lax.dot_general(x, y, dims, preferred_element_type=F32)

    return dot(a[0], b[0]) + (dot(a[0], b[1]) + dot(a[1], b[0]))


def spline_rows(frac):
    inner = 1.0 - frac
    square = frac * frac
    cube = square * frac
    return [
        inner * inner * inner * (1.0 / 6.0),
        (3.0 * cube - 6.0 * square + 4.0) * (1.0 / 6.0),
        (-3.0 * cube + 3.0 * square + 3.0 * frac + 1.0) * (1.0 / 6.0),
        cube * (1.0 / 6.0),
    ]


def hot(t, weights):
    out = jnp.where(t == 0, weights[0], 0.0)
    for step in range(1, 4):
        out = jnp.where(t == step, weights[step], out)
    return out


def turned(value, sign):
    lane = lax.broadcasted_iota(jnp.int32, (1, C), 1)
    factor = jnp.where(lane < C // 2, sign, -sign).astype(F32)
    parts = [pltpu.roll(value[:, i : i + C], C // 2, 1) * factor for i in range(0, value.shape[1], C)]
    return jnp.concatenate(parts, 1)


def stacked(value, sign):
    return split(jnp.concatenate([value, turned(value, sign)], 0))


def shifted_slab(s, k):
    z, y, c = s // 8, (s // 2) % 4, s % 2
    dz, dy, dc = k // 8, (k // 2) % 4, k % 2
    return ((z + dz) % 8) * 8 + ((y + dy) % 4) * 2 + (c + dc) % 2


def signal(target):
    pl.semaphore_signal(pltpu.get_barrier_semaphore(), inc=1, device_id=target, device_id_type=MESH)


def atoms_kernel(own_ref, out_ref, send_sem, recv_sem):
    s, d = lax.axis_index("slab"), lax.axis_index("dom")
    nxt, prv = (s + 1) % N_SLAB, (s + N_SLAB - 1) % N_SLAB
    for i in range(N_DOM):
        e = (d + i) % N_DOM
        signal((nxt, e))
        signal((prv, e))
        if i:
            signal((s, e))
    pl.semaphore_wait(pltpu.get_barrier_semaphore(), 3 * N_DOM - 1)
    copies = []
    for i in range(N_DOM):
        for g in range(2):
            if i == 0 and g == 0:
                continue
            copies.append(
                pltpu.make_async_remote_copy(
                    own_ref,
                    out_ref.at[g, d],
                    send_sem.at[g, i],
                    recv_sem.at[g, i],
                    device_id=(nxt if g else s, (d + i) % N_DOM),
                    device_id_type=MESH,
                )
            )
    for copy in copies:
        copy.start()
    out_ref[0, d] = own_ref[...]
    for copy in copies:
        copy.wait()


def main_kernel(
    atoms_ref, finish_ref, green_hbm, fz_hbm, even_hbm, odd_hbm, back_even_hbm, back_odd_hbm,
    pot_ref, grad_ref,
    green, fz, even_m, odd_m, back_even, back_odd,
    hot_z, wy_tab, wx_tab, grid_even, grid_odd, send1, recv1, send2, recv2, acc_even, acc_odd, send3, recv3,
    parts, parts_in,
    load_sem, send_sem, r1, r2, r3, r4,
):
    s, d = lax.axis_index("slab"), lax.axis_index("dom")
    nxt, prv = (s + 1) % N_SLAB, (s + N_SLAB - 1) % N_SLAB
    right, left = (d + 1) % N_DOM, (d + N_DOM - 1) % N_DOM

    def greet(k, carry):
        signal((shifted_slab(s, k), d))
        return carry

    lax.fori_loop(1, N_SLAB, greet, 0)
    for i in range(1, N_DOM):
        signal((s, (d + i) % N_DOM))
    signal((nxt, right))
    signal((prv, left))

    loads = [
        pltpu.make_async_copy(src, dst, load_sem.at[i])
        for i, (src, dst) in enumerate(
            [
                (fz_hbm, fz),
                (even_hbm, even_m),
                (odd_hbm, odd_m),
                (green_hbm, green),
                (back_even_hbm, back_even),
                (back_odd_hbm, back_odd),
            ]
        )
    ]
    for load in loads:
        load.start()

    grid_even[...] = jnp.zeros_like(grid_even)
    grid_odd[...] = jnp.zeros_like(grid_odd)
    row_z = lax.broadcasted_iota(jnp.int32, (NZ, ATOMS), 0)
    row = lax.broadcasted_iota(jnp.int32, (ROWS + EXTRA, ATOMS), 0)
    half = ROWS // 2
    row_y = jnp.where(
        row < ROWS,
        2 * (row % half) + row // half,
        ROWS + 2 * ((row - ROWS) % (EXTRA // 2)) + (row - ROWS) // (EXTRA // 2),
    )
    row_x = lax.broadcasted_iota(jnp.int32, (8, ATOMS), 0)
    loads[0].wait()
    mine = pl.ds(pl.multiple_of(d * C, C), C)
    fz_mine = (fz[0, mine], fz[1, mine])

    def spread(n, carry):
        i, g = n // 2, n % 2
        e = (d + i) % N_DOM
        data = atoms_ref[g, e]
        whole = data[0:3].astype(jnp.int32)
        hz = split(hot((row_z - whole[2:3]) & (NZ - 1), spline_rows(data[5:6])))
        hot_z[n, 0] = hz[0]
        hot_z[n, 1] = hz[1]
        wx = hot(row_x - whole[0:1] + XD * g, spline_rows(data[3:4]))
        wx_tab[n] = wx
        wy = hot(row_y - whole[1:2], spline_rows(data[4:5]))
        lines = dot3(fz_mine, hz) * data[6:7]
        scaled = split(jnp.concatenate([lines * wx[p : p + 1] for p in range(XD)], 0))
        out = dot3(split(wy), scaled, NT)
        here = pl.ds(pl.multiple_of(e * half, half), half)
        after = pl.ds(pl.multiple_of(((e + 1) % N_DOM) * half, half), EXTRA // 2)
        grid_even[here, :] += out[:half]
        grid_odd[here, :] += out[half:ROWS]
        grid_even[after, :] += out[ROWS : ROWS + EXTRA // 2]
        grid_odd[after, :] += out[ROWS + EXTRA // 2 :]
        return carry

    lax.fori_loop(0, 2 * N_DOM, spread, 0)

    loads[1].wait()
    loads[2].wait()
    for pair in range(2):
        lanes = slice(2 * C * pair, 2 * C * (pair + 1))
        a = dot3((even_m[0], even_m[1]), stacked(grid_even[:, lanes], 1.0))
        b = dot3((odd_m[0], odd_m[1]), stacked(grid_odd[:, lanes], 1.0))
        for first, value in ((0, a + b), (N_SLAB // 2, a - b)):
            for q in range(2):
                send1[first : first + N_SLAB // 2, 2 * pair + q] = value[:, C * q : C * (q + 1)].reshape(
                    N_SLAB // 2, KY, C
                )

    pl.semaphore_wait(pltpu.get_barrier_semaphore(), N_SLAB - 1 + N_DOM - 1 + 2)

    def post1(k, carry):
        t = shifted_slab(s, k)
        pltpu.make_async_remote_copy(
            send1.at[t],
            recv1.at[s],
            send_sem.at[0],
            r1,
            device_id=(t, d),
            device_id_type=MESH,
        ).start()
        return carry

    lax.fori_loop(1, N_SLAB, post1, 0)
    natural = lax.broadcasted_iota(jnp.int32, (ROWS, ATOMS), 0)
    for g in range(2):
        for first, size, e in ((0, ROWS, d), (ROWS, 8, left)):
            data = atoms_ref[g, e]
            base = data[1:2].astype(jnp.int32)
            wy_tab[g, first : first + size] = hot(first + natural[:size] - base, spline_rows(data[4:5]))
    recv1[s] = send1[s]
    loads[3].wait()
    others = pl.ds(0, N_SLAB - 1)
    pltpu.make_async_copy(recv1.at[others], recv1.at[others], r1).wait()

    lane = lax.broadcasted_iota(jnp.int32, (1, C), 1)
    zero_bin = jnp.logical_and(lane % (C // 2) == 0, d == 0)
    scale = jnp.where(zero_bin, 1.0, 2.0).astype(F32) * (1.0 / (NX * NY * NZ))
    flat1 = recv1.reshape(NX * KY, C)
    for part in range(2):

        def along_x(pair, carry):
            t = 4 * part + 2 * pair
            value = jnp.concatenate([flat1[pl.ds(t + q, NX, stride=KY), :] for q in range(2)], 1)
            spec = dot3((even_m[0], even_m[1]), stacked(value, 1.0))
            factor = []
            for q in range(2):
                f = green[pl.ds(t + q, NX, stride=KY), :]
                factor.append(jnp.concatenate([f, f], 1) * scale)
            spec = spec * jnp.concatenate(factor, 1)
            out = dot3((even_m[0], even_m[1]), stacked(spec, -1.0))
            for q in range(2):
                send2[part, pl.ds(2 * pair + q, NX, stride=4), :] = out[:, C * q : C * (q + 1)]
            return carry

        lax.fori_loop(0, 2, along_x, 0)

        def post2(k, carry):
            t = shifted_slab(s, k)
            pltpu.make_async_remote_copy(
                send2.at[part, pl.ds(pl.multiple_of(t * 16, 16), 16)],
                recv2.at[part, pl.ds(pl.multiple_of(s * 16, 16), 16)],
                send_sem.at[1],
                r2.at[part],
                device_id=(t, d),
                device_id_type=MESH,
            ).start()
            return carry

        lax.fori_loop(1, N_SLAB, post2, 0)
        own = pl.ds(pl.multiple_of(s * 16, 16), 16)
        recv2[part, own, :] = send2[part, own, :]

    loads[4].wait()
    loads[5].wait()
    copies3 = []
    for part in range(2):
        rows = pl.ds(0, (N_SLAB - 1) * 16)
        pltpu.make_async_copy(recv2.at[part, rows], recv2.at[part, rows], r2.at[part]).wait()
        for pair in range(2):
            low, high = [], []
            for q in range(2):
                p = 2 * pair + q
                pick = [recv2[part, pl.ds(4 * p + t, N_SLAB, stride=16), :] for t in range(4)]
                low.append(jnp.concatenate([v[: N_SLAB // 2] for v in pick], 0))
                high.append(jnp.concatenate([v[N_SLAB // 2 :] for v in pick], 0))
            low, high = jnp.concatenate(low, 1), jnp.concatenate(high, 1)
            even = dot3((back_even[0, part], back_even[1, part]), stacked(low + high, -1.0))
            odd = dot3((back_odd[0, part], back_odd[1, part]), stacked(low - high, -1.0))
            if part == 0:
                acc_even[pair] = even
                acc_odd[pair] = odd
                continue
            even = even + acc_even[pair]
            odd = odd + acc_odd[pair]
            for q in range(2):
                lanes = slice(C * q, C * (q + 1))
                for e in range(N_DOM):
                    send3[pair, e, q, pl.ds(0, half, stride=2), :] = even[e * half : (e + 1) * half, lanes]
                    send3[pair, e, q, pl.ds(1, half, stride=2), :] = odd[e * half : (e + 1) * half, lanes]
            for i in range(1, N_DOM):
                e = (d + i) % N_DOM
                copy = pltpu.make_async_remote_copy(
                    send3.at[pair, e],
                    recv3.at[pair, d],
                    send_sem.at[2],
                    r3.at[pair],
                    device_id=(s, e),
                    device_id_type=MESH,
                )
                copy.start()
            recv3[pair, d] = send3[pair, d]

    totals = [jnp.zeros((1, ATOMS), F32) for _ in range(4)]
    for pair in range(2):
        three = pl.ds(0, N_DOM - 1)
        pltpu.make_async_copy(recv3.at[pair, three], recv3.at[pair, three], r3.at[pair]).wait()
        columns = jnp.concatenate([recv3[pair, e].reshape(2 * ROWS, C) for e in range(N_DOM)], 1)
        block = dot3(split(columns), (fz[0], fz[1]))
        for q in range(2):
            pot_ref[2 * pair + q] = block[q * ROWS : (q + 1) * ROWS]
        both = split(block)
        edge = split(jnp.concatenate([block[q * ROWS : q * ROWS + 8] for q in range(2)], 0))
        for g in range(2):
            u = dot3(both, (hot_z[g, 0], hot_z[g, 1]))
            v = dot3(edge, (hot_z[6 + g, 0], hot_z[6 + g, 1]))
            for q in range(2):
                p = 2 * pair + q
                here = jnp.sum(u[q * ROWS : (q + 1) * ROWS] * wy_tab[g, :ROWS], 0, keepdims=True)
                there = jnp.sum(v[q * 8 : (q + 1) * 8] * wy_tab[g, ROWS:], 0, keepdims=True)
                totals[2 * g] += here * wx_tab[g, p : p + 1]
                totals[2 * g + 1] += there * wx_tab[6 + g, p : p + 1]
    for n in range(1, 4):
        parts[n] = jnp.broadcast_to(totals[n], (8, ATOMS))
    for n, target in ((1, (s, left)), (2, (prv, d)), (3, (prv, left))):
        pltpu.make_async_remote_copy(
            parts.at[n], parts_in.at[n], send_sem.at[2 + n], r4.at[n], device_id=target, device_id_type=MESH
        ).start()
    for n in range(1, 4):
        pltpu.make_async_copy(parts_in.at[n], parts_in.at[n], r4.at[n]).wait()
    total = totals[0] + parts_in[1, 0:1] + parts_in[2, 0:1] + parts_in[3, 0:1]
    grad_ref[...] = finish_ref[...] * total

    pltpu.make_async_copy(send1.at[others], send1.at[others], send_sem.at[0]).wait()
    sent = pl.ds(0, (N_SLAB - 1) * 16)
    for part in range(2):
        pltpu.make_async_copy(send2.at[part, sent], send2.at[part, sent], send_sem.at[1]).wait()
    for pair in range(2):
        pltpu.make_async_copy(send3.at[pair, three], send3.at[pair, three], send_sem.at[2]).wait()
    for n in range(1, 4):
        pltpu.make_async_copy(parts.at[n], parts.at[n], send_sem.at[2 + n]).wait()


def per_device(base_cells, offsets, charges, bias_coupling, counts, green):
    alive = jnp.arange(ATOMS, dtype=jnp.int32) < counts[0]
    own = jnp.stack(
        [
            (base_cells[0] % XD).astype(F32),
            (base_cells[1] % ROWS).astype(F32),
            base_cells[2].astype(F32),
            offsets[0],
            offsets[1],
            offsets[2],
            jnp.where(alive, charges, 0.0),
            jnp.zeros_like(charges),
        ]
    )
    vmem = pl.BlockSpec(memory_space=pltpu.VMEM)
    anywhere = pl.BlockSpec(memory_space=pl.ANY)
    atoms = pl.pallas_call(
        atoms_kernel,
        out_shape=jax.ShapeDtypeStruct((2, N_DOM, 8, ATOMS), F32),
        in_specs=[vmem],
        out_specs=vmem,
        scratch_shapes=[pltpu.SemaphoreType.DMA((2, N_DOM)), pltpu.SemaphoreType.DMA((2, N_DOM))],
        compiler_params=pltpu.CompilerParams(collective_id=1, has_side_effects=True),
        name="atoms",
    )(own)
    finish = jnp.broadcast_to(jnp.where(alive, bias_coupling, 0.0)[None], (1, ATOMS))
    tables = [jnp.asarray(t) for t in constants()]
    potential, gradient = pl.pallas_call(
        main_kernel,
        out_shape=(
            jax.ShapeDtypeStruct((XD, ROWS, NZ), F32),
            jax.ShapeDtypeStruct((1, ATOMS), F32),
        ),
        in_specs=[vmem, vmem] + [anywhere] * 6,
        out_specs=(vmem, vmem),
        scratch_shapes=[
            pltpu.VMEM((NX * KY, C // 2), F32),
            *[pltpu.VMEM(t.shape, BF16) for t in tables],
            pltpu.VMEM((2 * N_DOM, 2, NZ, ATOMS), BF16),
            pltpu.VMEM((2, ROWS + 8, ATOMS), F32),
            pltpu.VMEM((2 * N_DOM, 8, ATOMS), F32),
            pltpu.VMEM((NY // 2, XD * C), F32),
            pltpu.VMEM((NY // 2, XD * C), F32),
            pltpu.VMEM((N_SLAB, XD, KY, C), F32),
            pltpu.VMEM((N_SLAB, XD, KY, C), F32),
            pltpu.VMEM((2, N_SLAB * 16, C), F32),
            pltpu.VMEM((2, N_SLAB * 16, C), F32),
            pltpu.VMEM((2, NY // 2, 2 * C), F32),
            pltpu.VMEM((2, NY // 2, 2 * C), F32),
            pltpu.VMEM((2, N_DOM, 2, ROWS, C), F32),
            pltpu.VMEM((2, N_DOM, 2, ROWS, C), F32),
            pltpu.VMEM((4, 8, ATOMS), F32),
            pltpu.VMEM((4, 8, ATOMS), F32),
            pltpu.SemaphoreType.DMA((6,)),
            pltpu.SemaphoreType.DMA((6,)),
            pltpu.SemaphoreType.DMA,
            pltpu.SemaphoreType.DMA((2,)),
            pltpu.SemaphoreType.DMA((2,)),
            pltpu.SemaphoreType.DMA((4,)),
        ],
        compiler_params=pltpu.CompilerParams(
            collective_id=2, has_side_effects=True, vmem_limit_bytes=48 * 1024 * 1024
        ),
        name="mesh",
    )(atoms, finish, green.reshape(NX * KY, C // 2), *tables)
    return (potential, gradient.reshape(ATOMS))


def solution(mesh):
    placed = (
        P(None, ("slab", "dom")),
        P(None, ("slab", "dom")),
        P(("slab", "dom")),
        P(("slab", "dom")),
        P(("slab", "dom")),
        P(None, "slab", "dom"),
    )
    return jax.shard_map(
        per_device,
        mesh=mesh,
        in_specs=placed,
        out_specs=(P("slab", "dom", None), P(("slab", "dom"))),
        check_vma=False,
    )
```

```python
import functools

import numpy as np
import jax
import jax.numpy as jnp
from jax import lax
from jax.experimental import pallas as pl
from jax.experimental.pallas import tpu as pltpu
from jax.sharding import PartitionSpec as P

XD = 4
NY = 512
NZ = 512
NX = 256
N_SLAB = 64
N_DOM = 4
ROWS = NY // N_DOM
KY = NY // N_SLAB
ATOMS = 256
C = 128
MESH = pl.DeviceIdType.MESH
F32 = jnp.float32
BF16 = jnp.bfloat16
CHUNK = 1
CHUNKS = XD // CHUNK
EXTRA = 16


def halves(table):
    table = np.asarray(table, np.float32)
    high = table.astype(jnp.bfloat16)
    low = (table - high.astype(np.float32)).astype(jnp.bfloat16)
    return np.stack([high, low])


def constants():
    kz_local = NZ // 2 // N_DOM
    kz = np.arange(NZ // 2)
    angle = 2 * np.pi * ((kz[:, None] * np.arange(NZ)[None, :]) % NZ) / NZ
    fz = np.stack([np.cos(angle).reshape(N_DOM, kz_local, NZ), -np.sin(angle).reshape(N_DOM, kz_local, NZ)], 1)
    fz = fz.reshape(2 * kz_local * N_DOM, NZ)
    k = np.arange(256)
    even = 2 * np.pi * ((k[:, None] * k[None, :]) % 256) / 256
    odd = 2 * np.pi * ((k[:, None] * (2 * k[None, :] + 1)) % 512) / 512
    cs_even = np.concatenate([np.cos(even), np.sin(even)], 1)
    cs_odd = np.concatenate([np.cos(odd), np.sin(odd)], 1)
    cs_odd_t = np.concatenate([np.cos(odd).T, np.sin(odd).T], 1)
    return halves(np.concatenate([fz, cs_even, cs_odd, cs_odd_t], 0))


def split(value):
    high = value.astype(BF16)
    low = (value - high.astype(F32)).astype(BF16)
    return high, low


NN = (((1,), (0,)), ((), ()))
NT = (((1,), (1,)), ((), ()))


def dot3(a, b, dims=NN):
    def dot(x, y):
        return lax.dot_general(x, y, dims, preferred_element_type=F32)

    return dot(a[0], b[0]) + (dot(a[0], b[1]) + dot(a[1], b[0]))


def spline_rows(frac):
    inner = 1.0 - frac
    square = frac * frac
    cube = square * frac
    return [
        inner * inner * inner * (1.0 / 6.0),
        (3.0 * cube - 6.0 * square + 4.0) * (1.0 / 6.0),
        (-3.0 * cube + 3.0 * square + 3.0 * frac + 1.0) * (1.0 / 6.0),
        cube * (1.0 / 6.0),
    ]


def hot(t, weights):
    out = jnp.where(t == 0, weights[0], 0.0)
    for step in range(1, 4):
        out = jnp.where(t == step, weights[step], out)
    return out


def turned(value, sign):
    lane = lax.broadcasted_iota(jnp.int32, (1, C), 1)
    factor = jnp.where(lane < C // 2, sign, -sign).astype(F32)
    parts = [pltpu.roll(value[:, i : i + C], C // 2, 1) * factor for i in range(0, value.shape[1], C)]
    return jnp.concatenate(parts, 1)


def stacked(value, sign):
    return split(jnp.concatenate([value, turned(value, sign)], 0))


def shifted_slab(s, k):
    z, y, c = s // 8, (s // 2) % 4, s % 2
    dz, dy, dc = k // 8, (k // 2) % 4, k % 2
    return ((z + dz) % 8) * 8 + ((y + dy) % 4) * 2 + (c + dc) % 2


def signal(target):
    pl.semaphore_signal(pltpu.get_barrier_semaphore(), inc=1, device_id=target, device_id_type=MESH)


def main_kernel(
    counts_ref, cells_ref, offsets_ref, charges_ref, bias_ref, green_hbm, table_hbm,
    pot_ref, grad_ref,
    green, fz, even_m, odd_m, back_odd,
    own_ref, atoms_ref, factors, by_plane,
    hot_z, wy_tab, wx_tab, grid_even, grid_odd, send1, recv1, spectrum, send2, recv2, send3, recv3,
    totals, parts, parts_in,
    load_sem, send_sem, atom_send, atom_recv, r1, r2, r3, r4,
):
    s, d = lax.axis_index("slab"), lax.axis_index("dom")
    nxt, prv = (s + 1) % N_SLAB, (s + N_SLAB - 1) % N_SLAB
    right, left = (d + 1) % N_DOM, (d + N_DOM - 1) % N_DOM

    def greet(k, carry):
        signal((shifted_slab(s, k), d))
        return carry

    for i in range(1, N_DOM):
        signal((s, (d + i) % N_DOM))
        signal((nxt, (d + i) % N_DOM))
        signal((prv, (d + i) % N_DOM))
    lax.fori_loop(1, N_SLAB, greet, 0)

    loads = [
        pltpu.make_async_copy(src, dst, load_sem.at[i])
        for i, (src, dst) in enumerate(
            [
                (table_hbm.at[:, 0:NZ], fz),
                (table_hbm.at[:, NZ : NZ + NX], even_m),
                (table_hbm.at[:, NZ + NX : NZ + 2 * NX], odd_m),
                (green_hbm, green),
                (table_hbm.at[:, NZ + 2 * NX : NZ + 3 * NX], back_odd),
            ]
        )
    ]
    for load in loads:
        load.start()

    slot = lax.broadcasted_iota(jnp.int32, (1, ATOMS), 1)
    alive = slot < counts_ref[0]
    own_ref[0:1] = (cells_ref[0:1] % XD).astype(F32)
    own_ref[1:2] = (cells_ref[1:2] % ROWS).astype(F32)
    own_ref[2:3] = cells_ref[2:3].astype(F32)
    own_ref[3:6] = offsets_ref[...]
    own_ref[6:7] = jnp.where(alive, charges_ref[...], 0.0)
    own_ref[7:8] = jnp.zeros((1, ATOMS), F32)
    atoms_ref[0, d] = own_ref[...]
    grid_even[...] = jnp.zeros_like(grid_even)
    grid_odd[...] = jnp.zeros_like(grid_odd)
    totals[...] = jnp.zeros_like(totals)

    loads[1].wait()
    r = lax.broadcasted_iota(jnp.int32, (NX, NX), 0)
    x = lax.broadcasted_iota(jnp.int32, (NX, NX), 1)
    per = N_SLAB * CHUNK
    chosen = XD * ((r % per) // CHUNK) + CHUNK * (r // per) + r % CHUNK
    pick = jnp.where(x == chosen, 1.0, 0.0).astype(BF16)
    for n in range(2):
        by_plane[n] = lax.dot_general(pick, even_m[n], NN, preferred_element_type=F32).astype(BF16)

    loads[3].wait()
    lane = lax.broadcasted_iota(jnp.int32, (1, C), 1)
    zero_bin = jnp.logical_and(lane % (C // 2) == 0, d == 0)
    scale = jnp.where(zero_bin, 1.0, 2.0).astype(F32) * (1.0 / (NX * NY * NZ))

    def prepare(t, carry):
        f = green[t]
        factors[t] = jnp.concatenate([f, f], 0).T * scale
        return carry

    lax.fori_loop(0, KY, prepare, 0)

    pl.semaphore_wait(pltpu.get_barrier_semaphore(), N_SLAB - 1 + 3 * (N_DOM - 1))

    for g in range(2):
        for i in range(N_DOM):
            if i == 0 and g == 0:
                continue
            pltpu.make_async_remote_copy(
                own_ref,
                atoms_ref.at[g, d],
                atom_send,
                atom_recv.at[g, i],
                device_id=(nxt if g else s, (d + i) % N_DOM),
                device_id_type=MESH,
            ).start()

    row_z = lax.broadcasted_iota(jnp.int32, (NZ, ATOMS), 0)
    row = lax.broadcasted_iota(jnp.int32, (ROWS + EXTRA, ATOMS), 0)
    half = ROWS // 2
    row_y = jnp.where(
        row < ROWS,
        2 * (row % half) + row // half,
        ROWS + 2 * ((row - ROWS) % (EXTRA // 2)) + (row - ROWS) // (EXTRA // 2),
    )
    row_x = lax.broadcasted_iota(jnp.int32, (8, ATOMS), 0)
    loads[0].wait()
    mine = pl.ds(pl.multiple_of(d * C, C), C)
    fz_mine = (fz[0, mine], fz[1, mine])

    def spread(n, carry):
        i, g = n // 2, n % 2
        e = (d + i) % N_DOM

        @pl.when(n > 0)
        def _():
            block = atoms_ref.at[g, e]
            pltpu.make_async_copy(block, block, atom_recv.at[g, (N_DOM - i) % N_DOM]).wait()

        data = atoms_ref[g, e]
        whole = data[0:3].astype(jnp.int32)
        hz = split(hot((row_z - whole[2:3]) & (NZ - 1), spline_rows(data[5:6])))
        hot_z[n, 0] = hz[0]
        hot_z[n, 1] = hz[1]
        wx = hot(row_x - whole[0:1] + XD * g, spline_rows(data[3:4]))
        wx_tab[n] = wx
        wy = hot(row_y - whole[1:2], spline_rows(data[4:5]))
        lines = dot3(fz_mine, hz) * data[6:7]
        scaled = split(jnp.concatenate([lines * wx[p : p + 1] for p in range(XD)], 0))
        out = dot3(split(wy), scaled, NT)
        here = pl.ds(pl.multiple_of(e * half, half), half)
        after = pl.ds(pl.multiple_of(((e + 1) % N_DOM) * half, half), EXTRA // 2)
        grid_even[here, :] += out[:half]
        grid_odd[here, :] += out[half:ROWS]
        grid_even[after, :] += out[ROWS : ROWS + EXTRA // 2]
        grid_odd[after, :] += out[ROWS + EXTRA // 2 :]
        return carry

    lax.fori_loop(0, 2 * N_DOM, spread, 0)

    loads[2].wait()
    for pair in range(2):
        lanes = slice(2 * C * pair, 2 * C * (pair + 1))
        a = dot3((even_m[0], even_m[1]), stacked(grid_even[:, lanes], 1.0))
        b = dot3((odd_m[0], odd_m[1]), stacked(grid_odd[:, lanes], 1.0))
        for first, value in ((0, a + b), (N_SLAB // 2, a - b)):
            for q in range(2):
                send1[first : first + N_SLAB // 2, 2 * pair + q] = value[:, C * q : C * (q + 1)].reshape(
                    N_SLAB // 2, KY, C
                )

    def post1(k, carry):
        t = shifted_slab(s, k)
        pltpu.make_async_remote_copy(
            send1.at[t], recv1.at[s], send_sem.at[0], r1, device_id=(t, d), device_id_type=MESH
        ).start()
        return carry

    lax.fori_loop(1, N_SLAB, post1, 0)
    natural = lax.broadcasted_iota(jnp.int32, (ROWS, ATOMS), 0)
    for g in range(2):
        for first, size, e in ((0, ROWS, d), (ROWS, 8, left)):
            data = atoms_ref[g, e]
            base = data[1:2].astype(jnp.int32)
            wy_tab[g, first : first + size] = hot(first + natural[:size] - base, spline_rows(data[4:5]))
    recv1[s] = send1[s]
    others = pl.ds(0, N_SLAB - 1)
    pltpu.make_async_copy(recv1.at[others], recv1.at[others], r1).wait()

    flat1 = recv1.reshape(NX * KY, C)
    for pair in range(KY // 2):
        value = jnp.concatenate([flat1[pl.ds(2 * pair + q, NX, stride=KY), :] for q in range(2)], 1)
        spec = dot3((even_m[0], even_m[1]), stacked(value, 1.0))
        spec = spec * jnp.concatenate([factors[2 * pair], factors[2 * pair + 1]], 1)
        high, low = stacked(spec, -1.0)
        spectrum[0, :, 2 * C * pair : 2 * C * (pair + 1)] = high
        spectrum[1, :, 2 * C * pair : 2 * C * (pair + 1)] = low

    flat2 = send2.reshape(CHUNKS, per * KY, C)

    def along_x(ch, carry):
        rows = pl.ds(pl.multiple_of(ch * per, per), per)
        out = dot3((by_plane[0, rows], by_plane[1, rows]), (spectrum[0], spectrum[1]))
        for t in range(KY):
            flat2[ch, pl.ds(t, per, stride=KY), :] = out[:, C * t : C * (t + 1)]

        def post2(k, inner):
            t = shifted_slab(s, k)
            pltpu.make_async_remote_copy(
                send2.at[ch, t],
                recv2.at[ch, s],
                send_sem.at[1],
                r2.at[ch],
                device_id=(t, d),
                device_id_type=MESH,
            ).start()
            return inner

        lax.fori_loop(1, N_SLAB, post2, 0)
        recv2[ch, s] = send2[ch, s]
        return carry

    lax.fori_loop(0, CHUNKS, along_x, 0)
    loads[4].wait()
    three = pl.ds(0, N_DOM - 1)

    def finish(ch, carry):
        @pl.when(ch < CHUNKS)
        def _():
            pltpu.make_async_copy(recv2.at[ch, others], recv2.at[ch, others], r2.at[ch]).wait()
            value = jnp.concatenate([recv2[ch, :, q].reshape(NY, C) for q in range(CHUNK)], 1)
            low, high = value[: NY // 2], value[NY // 2 :]
            even = dot3((even_m[0], even_m[1]), stacked(low + high, -1.0))
            odd = dot3((back_odd[0], back_odd[1]), stacked(low - high, -1.0))
            for q in range(CHUNK):
                lanes = slice(C * q, C * (q + 1))
                for e in range(N_DOM):
                    send3[ch, e, q, pl.ds(0, half, stride=2), :] = even[e * half : (e + 1) * half, lanes]
                    send3[ch, e, q, pl.ds(1, half, stride=2), :] = odd[e * half : (e + 1) * half, lanes]
            for i in range(1, N_DOM):
                e = (d + i) % N_DOM
                pltpu.make_async_remote_copy(
                    send3.at[ch, e],
                    recv3.at[ch, d],
                    send_sem.at[2],
                    r3.at[ch],
                    device_id=(s, e),
                    device_id_type=MESH,
                ).start()
            recv3[ch, d] = send3[ch, d]

        @pl.when(ch > 0)
        def _():
            c = ch - 1
            pltpu.make_async_copy(recv3.at[c, three], recv3.at[c, three], r3.at[c]).wait()
            columns = jnp.concatenate([recv3[c, e].reshape(CHUNK * ROWS, C) for e in range(N_DOM)], 1)
            block = dot3(split(columns), (fz[0], fz[1]))
            for q in range(CHUNK):
                pot_ref[CHUNK * c + q] = block[q * ROWS : (q + 1) * ROWS]
            both = split(block)
            edge = split(jnp.concatenate([block[q * ROWS : q * ROWS + 8] for q in range(CHUNK)], 0))
            for g in range(2):
                u = dot3(both, (hot_z[g, 0], hot_z[g, 1]))
                v = dot3(edge, (hot_z[6 + g, 0], hot_z[6 + g, 1]))
                for q in range(CHUNK):
                    p = CHUNK * c + q
                    here = jnp.sum(u[q * ROWS : (q + 1) * ROWS] * wy_tab[g, :ROWS], 0, keepdims=True)
                    there = jnp.sum(v[q * 8 : (q + 1) * 8] * wy_tab[g, ROWS:], 0, keepdims=True)
                    totals[2 * g] += here * wx_tab[g, pl.ds(p, 1)]
                    totals[2 * g + 1] += there * wx_tab[6 + g, pl.ds(p, 1)]

        return carry

    lax.fori_loop(0, CHUNKS + 1, finish, 0)

    for n in range(1, 4):
        parts[n] = jnp.broadcast_to(totals[n], (8, ATOMS))
    for n, target in ((1, (s, left)), (2, (prv, d)), (3, (prv, left))):
        pltpu.make_async_remote_copy(
            parts.at[n], parts_in.at[n], send_sem.at[2 + n], r4.at[n], device_id=target, device_id_type=MESH
        ).start()
    for n in range(1, 4):
        pltpu.make_async_copy(parts_in.at[n], parts_in.at[n], r4.at[n]).wait()
    total = totals[0] + parts_in[1, 0:1] + parts_in[2, 0:1] + parts_in[3, 0:1]
    grad_ref[...] = jnp.where(alive, bias_ref[...] * total, 0.0)

    seven = atoms_ref.reshape(2 * N_DOM, 8, ATOMS).at[pl.ds(0, 2 * N_DOM - 1)]
    pltpu.make_async_copy(seven, seven, atom_send).wait()
    pltpu.make_async_copy(send1.at[others], send1.at[others], send_sem.at[0]).wait()

    def drain(ch, carry):
        pltpu.make_async_copy(send2.at[ch, others], send2.at[ch, others], send_sem.at[1]).wait()
        pltpu.make_async_copy(send3.at[ch, three], send3.at[ch, three], send_sem.at[2]).wait()
        return carry

    lax.fori_loop(0, CHUNKS, drain, 0)
    for n in range(1, 4):
        pltpu.make_async_copy(parts.at[n], parts.at[n], send_sem.at[2 + n]).wait()


def per_device(base_cells, offsets, charges, bias_coupling, counts, green):
    vmem = pl.BlockSpec(memory_space=pltpu.VMEM)
    hbm = pl.BlockSpec(memory_space=pltpu.HBM)
    potential, gradient = pl.pallas_call(
        main_kernel,
        out_shape=(
            jax.ShapeDtypeStruct((XD, ROWS, NZ), F32),
            jax.ShapeDtypeStruct((1, ATOMS), F32),
        ),
        in_specs=[pl.BlockSpec(memory_space=pltpu.SMEM)] + [vmem] * 4 + [hbm] * 2,
        out_specs=(vmem, vmem),
        scratch_shapes=[
            pltpu.VMEM((KY, C // 2, NX), F32),
            pltpu.VMEM((2, NZ, NZ), BF16),
            pltpu.VMEM((2, NX, 2 * NX), BF16),
            pltpu.VMEM((2, NX, 2 * NX), BF16),
            pltpu.VMEM((2, NX, 2 * NX), BF16),
            pltpu.VMEM((8, ATOMS), F32),
            pltpu.VMEM((2, N_DOM, 8, ATOMS), F32),
            pltpu.VMEM((KY, NX, C), F32),
            pltpu.VMEM((2, NX, 2 * NX), BF16),
            pltpu.VMEM((2 * N_DOM, 2, NZ, ATOMS), BF16),
            pltpu.VMEM((2, ROWS + 8, ATOMS), F32),
            pltpu.VMEM((2 * N_DOM, 8, ATOMS), F32),
            pltpu.VMEM((NY // 2, XD * C), F32),
            pltpu.VMEM((NY // 2, XD * C), F32),
            pltpu.VMEM((N_SLAB, XD, KY, C), F32),
            pltpu.VMEM((N_SLAB, XD, KY, C), F32),
            pltpu.VMEM((2, 2 * NX, KY * C), BF16),
            pltpu.VMEM((CHUNKS, N_SLAB, CHUNK, KY, C), F32),
            pltpu.VMEM((CHUNKS, N_SLAB, CHUNK, KY, C), F32),
            pltpu.VMEM((CHUNKS, N_DOM, CHUNK, ROWS, C), F32),
            pltpu.VMEM((CHUNKS, N_DOM, CHUNK, ROWS, C), F32),
            pltpu.VMEM((4, 1, ATOMS), F32),
            pltpu.VMEM((4, 8, ATOMS), F32),
            pltpu.VMEM((4, 8, ATOMS), F32),
            pltpu.SemaphoreType.DMA((5,)),
            pltpu.SemaphoreType.DMA((6,)),
            pltpu.SemaphoreType.DMA,
            pltpu.SemaphoreType.DMA((2, N_DOM)),
            pltpu.SemaphoreType.DMA,
            pltpu.SemaphoreType.DMA((CHUNKS,)),
            pltpu.SemaphoreType.DMA((CHUNKS,)),
            pltpu.SemaphoreType.DMA((4,)),
        ],
        compiler_params=pltpu.CompilerParams(
            collective_id=1, has_side_effects=True, vmem_limit_bytes=53_000_000
        ),
        name="mesh",
    )(
        counts,
        base_cells,
        offsets,
        charges.reshape(1, ATOMS),
        bias_coupling.reshape(1, ATOMS),
        green.transpose(1, 2, 0),
        jnp.asarray(constants()),
    )
    return (potential, gradient.reshape(ATOMS))


def solution(mesh):
    placed = (
        P(None, ("slab", "dom")),
        P(None, ("slab", "dom")),
        P(("slab", "dom")),
        P(("slab", "dom")),
        P(("slab", "dom")),
        P(None, "slab", "dom"),
    )
    return jax.shard_map(
        per_device,
        mesh=mesh,
        in_specs=placed,
        out_specs=(P("slab", "dom", None), P(("slab", "dom"))),
        check_vma=False,
    )
```

```python
import functools

import numpy as np
import jax
import jax.numpy as jnp
from jax import lax
from jax.experimental import pallas as pl
from jax.experimental.pallas import tpu as pltpu
from jax.sharding import PartitionSpec as P

XD = 4
NY = 512
NZ = 512
NX = 256
N_SLAB = 64
N_DOM = 4
ROWS = NY // N_DOM
KY = NY // N_SLAB
ATOMS = 256
C = 128
MESH = pl.DeviceIdType.MESH
F32 = jnp.float32
BF16 = jnp.bfloat16
CHUNK = 1
CHUNKS = XD // CHUNK
EXTRA = 16


def halves(table):
    table = np.asarray(table, np.float32)
    high = table.astype(jnp.bfloat16)
    low = (table - high.astype(np.float32)).astype(jnp.bfloat16)
    return np.stack([high, low])


def constants():
    kz_local = NZ // 2 // N_DOM
    kz = np.arange(NZ // 2)
    angle = 2 * np.pi * ((kz[:, None] * np.arange(NZ)[None, :]) % NZ) / NZ
    fz = np.stack([np.cos(angle).reshape(N_DOM, kz_local, NZ), -np.sin(angle).reshape(N_DOM, kz_local, NZ)], 1)
    fz = fz.reshape(2 * kz_local * N_DOM, NZ)
    k = np.arange(256)
    even = 2 * np.pi * ((k[:, None] * k[None, :]) % 256) / 256
    odd = 2 * np.pi * ((k[:, None] * (2 * k[None, :] + 1)) % 512) / 512
    cs_even = np.concatenate([np.cos(even), np.sin(even)], 1)
    cs_odd = np.concatenate([np.cos(odd), np.sin(odd)], 1)
    cs_odd_t = np.concatenate([np.cos(odd).T, np.sin(odd).T], 1)
    main = halves(np.concatenate([fz, cs_even, cs_odd, cs_odd_t], 0))
    coarse, fine = halves(fz[:, ::16]), halves(fz[:, :32])
    blank = np.zeros((NZ, 64), jnp.bfloat16)
    pair = np.concatenate([coarse[0], coarse[1], blank, fine[0], fine[0], fine[1], blank[:, :32]], 1)
    pair = pair.reshape(2, 2, C, 256).transpose(0, 2, 1, 3).reshape(2, C, 512)
    return np.concatenate([main, pair], 1)


def split(value):
    high = value.astype(BF16)
    low = (value - high.astype(F32)).astype(BF16)
    return high, low


NN = (((1,), (0,)), ((), ()))
NT = (((1,), (1,)), ((), ()))


def dot3(a, b, dims=NN):
    def dot(x, y):
        return lax.dot_general(x, y, dims, preferred_element_type=F32)

    return dot(a[0], b[0]) + (dot(a[0], b[1]) + dot(a[1], b[0]))


def spline_rows(frac):
    inner = 1.0 - frac
    square = frac * frac
    cube = square * frac
    return [
        inner * inner * inner * (1.0 / 6.0),
        (3.0 * cube - 6.0 * square + 4.0) * (1.0 / 6.0),
        (-3.0 * cube + 3.0 * square + 3.0 * frac + 1.0) * (1.0 / 6.0),
        cube * (1.0 / 6.0),
    ]


def hot(t, weights):
    out = jnp.where(t == 0, weights[0], 0.0)
    for step in range(1, 4):
        out = jnp.where(t == step, weights[step], out)
    return out


def turned(value, sign):
    lane = lax.broadcasted_iota(jnp.int32, (1, C), 1)
    factor = jnp.where(lane < C // 2, sign, -sign).astype(F32)
    parts = [pltpu.roll(value[:, i : i + C], C // 2, 1) * factor for i in range(0, value.shape[1], C)]
    return jnp.concatenate(parts, 1)


def stacked(value, sign):
    return split(jnp.concatenate([value, turned(value, sign)], 0))


def shifted_slab(s, k):
    z, y, c = s // 8, (s // 2) % 4, s % 2
    dz, dy, dc = k // 8, (k // 2) % 4, k % 2
    return ((z + dz) % 8) * 8 + ((y + dy) % 4) * 2 + (c + dc) % 2


FAR = N_SLAB // 2
SENDS = ((0, 0, 0), (0, 1, 1), (1, 0, FAR), (1, 1, FAR + 1))
AWAY = (0, 1, N_SLAB - 1, FAR, FAR + 1, FAR - 1)


def near_plane(z, m):
    first = z + 7 - z % 2
    return (first + (m + 64 - first) % 4) % 8


def signal(target):
    pl.semaphore_signal(pltpu.get_barrier_semaphore(), inc=1, device_id=target, device_id_type=MESH)


def main_kernel(
    counts_ref, cells_ref, offsets_ref, charges_ref, green_hbm, table_hbm,
    pot_hbm, grad_ref,
    green, fz, even_m, odd_m, back_odd, phases,
    own_ref, atoms_ref, factors, by_plane,
    hot_z, wy_tab, wx_tab, grid_even, grid_odd, send1, recv1, spectrum, send2, recv2, send3, recv3,
    pot_ref, totals, parts, parts_in,
    load_sem, pot_sem, send_sem, atom_send, atom_recv, r1, r2, r3, r4,
):
    s, d = lax.axis_index("slab"), lax.axis_index("dom")
    nxt, prv = (s + 1) % N_SLAB, (s + N_SLAB - 1) % N_SLAB
    right, left = (d + 1) % N_DOM, (d + N_DOM - 1) % N_DOM

    def greet(k, carry):
        signal((shifted_slab(s, k), d))
        return carry

    for i in range(1, N_DOM):
        for step in AWAY:
            signal(((s + step) % N_SLAB, (d + i) % N_DOM))
    lax.fori_loop(1, N_SLAB, greet, 0)

    loads = [
        pltpu.make_async_copy(src, dst, load_sem.at[i])
        for i, (src, dst) in enumerate(
            [
                (table_hbm.at[:, 0:NZ], fz),
                (table_hbm.at[:, NZ : NZ + NX], even_m),
                (table_hbm.at[:, NZ + NX : NZ + 2 * NX], odd_m),
                (green_hbm, green),
                (table_hbm.at[:, NZ + 2 * NX : NZ + 3 * NX], back_odd),
                (
                    table_hbm.at[d // 2, pl.ds(NZ + 3 * NX, C), pl.ds(pl.multiple_of((d % 2) * 256, 256), 256)],
                    phases,
                ),
            ]
        )
    ]
    for load in loads:
        load.start()

    slot = lax.broadcasted_iota(jnp.int32, (1, ATOMS), 1)
    alive = slot < counts_ref[0]
    own_ref[0:1] = (cells_ref[0:1] % XD).astype(F32)
    own_ref[1:2] = (cells_ref[1:2] % ROWS).astype(F32)
    own_ref[2:3] = cells_ref[2:3].astype(F32)
    own_ref[3:6] = offsets_ref[...]
    own_ref[6:7] = jnp.where(alive, charges_ref[...], 0.0)
    own_ref[7:8] = jnp.zeros((1, ATOMS), F32)
    atoms_ref[0, 0, d] = own_ref[...]
    grid_even[...] = jnp.zeros_like(grid_even)
    grid_odd[...] = jnp.zeros_like(grid_odd)
    totals[...] = jnp.zeros_like(totals)

    loads[1].wait()
    r = lax.broadcasted_iota(jnp.int32, (NX, NX), 0)
    x = lax.broadcasted_iota(jnp.int32, (NX, NX), 1)
    per = N_SLAB * CHUNK
    chosen = XD * ((r % per) // CHUNK) + CHUNK * (r // per) + r % CHUNK
    pick = jnp.where(x == chosen, 1.0, 0.0).astype(BF16)
    for n in range(2):
        by_plane[n] = lax.dot_general(pick, even_m[n], NN, preferred_element_type=F32).astype(BF16)

    loads[3].wait()
    lane = lax.broadcasted_iota(jnp.int32, (1, C), 1)
    zero_bin = jnp.logical_and(lane % (C // 2) == 0, d == 0)
    scale = jnp.where(zero_bin, 1.0, 2.0).astype(F32)

    def prepare(t, carry):
        f = green[t]
        factors[t] = jnp.concatenate([f, f], 0).T * scale
        return carry

    lax.fori_loop(0, KY, prepare, 0)

    pl.semaphore_wait(pltpu.get_barrier_semaphore(), N_SLAB - 1 + len(AWAY) * (N_DOM - 1))

    for h, g, step in SENDS:
        for i in range(N_DOM):
            if h == g == i == 0:
                continue
            pltpu.make_async_remote_copy(
                own_ref,
                atoms_ref.at[h, g, d],
                atom_send,
                atom_recv.at[h, g, i],
                device_id=((s + step) % N_SLAB, (d + i) % N_DOM),
                device_id_type=MESH,
            ).start()

    row_h = lax.broadcasted_iota(jnp.int32, (64, ATOMS), 0) % 32
    row_l = lax.broadcasted_iota(jnp.int32, (32, ATOMS), 0)
    row = lax.broadcasted_iota(jnp.int32, (ROWS + EXTRA, ATOMS), 0)
    half = ROWS // 2
    row_y = jnp.where(
        row < ROWS,
        2 * (row % half) + row // half,
        ROWS + 2 * ((row - ROWS) % (EXTRA // 2)) + (row - ROWS) // (EXTRA // 2),
    )
    row_x = lax.broadcasted_iota(jnp.int32, (8, ATOMS), 0)
    loads[5].wait()

    z, inner = s // 8, s % 8
    served = near_plane(z, lax.broadcasted_iota(jnp.int32, (NX, 2 * C), 0) // 64)
    sign = jnp.where(served < 4, 1.0, -1.0).astype(F32)
    here = (z % 4) * 8 + inner
    loads[2].wait()

    def spread(i, h):
        e = (d + i) % N_DOM
        rows_y, scaled = [], []
        for g in range(2):

            def arrive():
                block = atoms_ref.at[h, g, e]
                pltpu.make_async_copy(block, block, atom_recv.at[h, g, (N_DOM - i) % N_DOM]).wait()

            if g == 0:
                pl.when(h + i > 0)(arrive)
            else:
                arrive()
            data = atoms_ref[h, g, e]
            whole = data[0:3].astype(jnp.int32)
            cell = whole[2:3]
            coarse = jnp.where(row_h == cell // 16, 1.0, 0.0).astype(BF16)
            fine = split(hot(row_l - cell % 16, spline_rows(data[5:6])))
            a = jnp.dot(phases[:, :64], coarse, preferred_element_type=F32)
            b = jnp.dot(
                phases[:, C : C + 96],
                jnp.concatenate([fine[0], fine[1], fine[0]], 0),
                preferred_element_type=F32,
            )
            a_re, a_im, b_re, b_im = a[: C // 2], a[C // 2 :], b[: C // 2], b[C // 2 :]
            lines = jnp.concatenate([a_re * b_re - a_im * b_im, a_re * b_im + a_im * b_re], 0) * data[6:7]
            wx = hot(row_x - whole[0:1] + XD * g, spline_rows(data[3:4]))
            rows_y.append(hot(row_y - whole[1:2], spline_rows(data[4:5])))
            scaled.append(jnp.concatenate([lines * wx[p : p + 1] for p in range(XD)], 0))
        out = dot3(split(jnp.concatenate(rows_y, 1)), split(jnp.concatenate(scaled, 1)), NT)
        own_rows = pl.ds(pl.multiple_of(e * half, half), half)
        after = pl.ds(pl.multiple_of(((e + 1) % N_DOM) * half, half), EXTRA // 2)
        grid_even[h, own_rows, :] += out[:half]
        grid_odd[h, own_rows, :] += out[half:ROWS]
        grid_even[h, after, :] += out[ROWS : ROWS + EXTRA // 2]
        grid_odd[h, after, :] += out[ROWS + EXTRA // 2 :]
        return h

    def outward(h, carry):
        lax.fori_loop(0, N_DOM, spread, h)
        for pair in range(2):
            lanes = slice(2 * C * pair, 2 * C * (pair + 1))
            a = dot3((even_m[0], even_m[1]), stacked(grid_even[h, :, lanes], 1.0))
            b = dot3((odd_m[0], odd_m[1]), stacked(grid_odd[h, :, lanes], 1.0))
            value = a + sign * b
            for q in range(2):
                send1[:, h, 2 * pair + q] = value[:, C * q : C * (q + 1)].reshape(FAR, KY, C)

        def post1(k, inside):
            j = (here + k) % FAR
            t = near_plane(z, j // 8) * 8 + j % 8
            pltpu.make_async_remote_copy(
                send1.at[j, h],
                recv1.at[(s + FAR * h) % N_SLAB],
                send_sem.at[0],
                r1,
                device_id=(t, d),
                device_id_type=MESH,
            ).start()
            return inside

        lax.fori_loop(1, FAR, post1, 0)
        return carry

    lax.fori_loop(0, 2, outward, 0)
    for h in range(2):
        recv1[(s + FAR * h) % N_SLAB] = send1[here, h]
    natural = lax.broadcasted_iota(jnp.int32, (ROWS, ATOMS), 0)
    row_z = lax.broadcasted_iota(jnp.int32, (NZ, ATOMS), 0)
    for g in range(2):
        for n, first, size, e in ((0, 0, ROWS, d), (1, ROWS, 8, left)):
            data = atoms_ref[0, g, e]
            whole = data[0:3].astype(jnp.int32)
            wy_tab[g, first : first + size] = hot(first + natural[:size] - whole[1:2], spline_rows(data[4:5]))
            wx_tab[2 * n + g] = hot(row_x - whole[0:1] + XD * g, spline_rows(data[3:4]))
            hz = split(hot((row_z - whole[2:3]) & (NZ - 1), spline_rows(data[5:6])))
            hot_z[2 * n + g, 0] = hz[0]
            hot_z[2 * n + g, 1] = hz[1]
    others = pl.ds(0, N_SLAB - 1)
    sent1 = pl.ds(0, N_SLAB - 2)
    pltpu.make_async_copy(recv1.at[sent1], recv1.at[sent1], r1).wait()

    flat1 = recv1.reshape(NX * KY, C)
    for pair in range(KY // 2):
        value = jnp.concatenate([flat1[pl.ds(2 * pair + q, NX, stride=KY), :] for q in range(2)], 1)
        spec = dot3((even_m[0], even_m[1]), stacked(value, 1.0))
        spec = spec * jnp.concatenate([factors[2 * pair], factors[2 * pair + 1]], 1)
        high, low = stacked(spec, -1.0)
        spectrum[0, :, 2 * C * pair : 2 * C * (pair + 1)] = high
        spectrum[1, :, 2 * C * pair : 2 * C * (pair + 1)] = low

    flat2 = send2.reshape(CHUNKS, per * KY, C)

    def along_x(ch, carry):
        rows = pl.ds(pl.multiple_of(ch * per, per), per)
        out = dot3((by_plane[0, rows], by_plane[1, rows]), (spectrum[0], spectrum[1]))
        for t in range(KY):
            flat2[ch, pl.ds(t, per, stride=KY), :] = out[:, C * t : C * (t + 1)]

        def post2(k, inner):
            t = shifted_slab(s, k)
            pltpu.make_async_remote_copy(
                send2.at[ch, t],
                recv2.at[ch, s],
                send_sem.at[1],
                r2.at[ch],
                device_id=(t, d),
                device_id_type=MESH,
            ).start()
            return inner

        lax.fori_loop(1, N_SLAB, post2, 0)
        recv2[ch, s] = send2[ch, s]
        return carry

    lax.fori_loop(0, CHUNKS, along_x, 0)
    loads[0].wait()
    loads[4].wait()
    three = pl.ds(0, N_DOM - 1)

    def finish(ch, carry):
        @pl.when(ch < CHUNKS)
        def _():
            pltpu.make_async_copy(recv2.at[ch, others], recv2.at[ch, others], r2.at[ch]).wait()
            value = jnp.concatenate([recv2[ch, :, q].reshape(NY, C) for q in range(CHUNK)], 1)
            low, high = value[: NY // 2], value[NY // 2 :]
            even = dot3((even_m[0], even_m[1]), stacked(low + high, -1.0))
            odd = dot3((back_odd[0], back_odd[1]), stacked(low - high, -1.0))
            for q in range(CHUNK):
                lanes = slice(C * q, C * (q + 1))
                for e in range(N_DOM):
                    send3[ch, e, q, pl.ds(0, half, stride=2), :] = even[e * half : (e + 1) * half, lanes]
                    send3[ch, e, q, pl.ds(1, half, stride=2), :] = odd[e * half : (e + 1) * half, lanes]
            for i in range(1, N_DOM):
                e = (d + i) % N_DOM
                pltpu.make_async_remote_copy(
                    send3.at[ch, e],
                    recv3.at[ch, d],
                    send_sem.at[2],
                    r3.at[ch],
                    device_id=(s, e),
                    device_id_type=MESH,
                ).start()
            recv3[ch, d] = send3[ch, d]

        @pl.when(ch > 0)
        def _():
            c = ch - 1
            pltpu.make_async_copy(recv3.at[c, three], recv3.at[c, three], r3.at[c]).wait()
            columns = jnp.concatenate([recv3[c, e].reshape(CHUNK * ROWS, C) for e in range(N_DOM)], 1)
            block = dot3(split(columns), (fz[0], fz[1]))
            for q in range(CHUNK):
                pot_ref[CHUNK * c + q] = block[q * ROWS : (q + 1) * ROWS]
            done = pl.ds(pl.multiple_of(CHUNK * c, CHUNK), CHUNK)
            pltpu.make_async_copy(pot_ref.at[done], pot_hbm.at[done], pot_sem).start()
            both = split(block)
            edge = split(jnp.concatenate([block[q * ROWS : q * ROWS + 8] for q in range(CHUNK)], 0))
            for g in range(2):
                u = dot3(both, (hot_z[g, 0], hot_z[g, 1]))
                v = dot3(edge, (hot_z[2 + g, 0], hot_z[2 + g, 1]))
                for q in range(CHUNK):
                    p = CHUNK * c + q
                    here = jnp.sum(u[q * ROWS : (q + 1) * ROWS] * wy_tab[g, :ROWS], 0, keepdims=True)
                    there = jnp.sum(v[q * 8 : (q + 1) * 8] * wy_tab[g, ROWS:], 0, keepdims=True)
                    totals[2 * g] += here * wx_tab[g, pl.ds(p, 1)]
                    totals[2 * g + 1] += there * wx_tab[2 + g, pl.ds(p, 1)]

        return carry

    lax.fori_loop(0, CHUNKS + 1, finish, 0)

    for n in range(1, 4):
        parts[n] = jnp.broadcast_to(totals[n], (8, ATOMS))
    for n, target in ((1, (s, left)), (2, (prv, d)), (3, (prv, left))):
        pltpu.make_async_remote_copy(
            parts.at[n], parts_in.at[n], send_sem.at[2 + n], r4.at[n], device_id=target, device_id_type=MESH
        ).start()
    for n in range(1, 4):
        pltpu.make_async_copy(parts_in.at[n], parts_in.at[n], r4.at[n]).wait()
    total = totals[0] + parts_in[1, 0:1] + parts_in[2, 0:1] + parts_in[3, 0:1]
    grad_ref[...] = total
    pltpu.make_async_copy(pot_ref, pot_hbm, pot_sem).wait()

    gone = atoms_ref.reshape(4 * N_DOM, 8, ATOMS).at[pl.ds(0, 4 * N_DOM - 1)]
    pltpu.make_async_copy(gone, gone, atom_send).wait()
    pltpu.make_async_copy(recv1.at[sent1], recv1.at[sent1], send_sem.at[0]).wait()

    def drain(ch, carry):
        pltpu.make_async_copy(send2.at[ch, others], send2.at[ch, others], send_sem.at[1]).wait()
        pltpu.make_async_copy(send3.at[ch, three], send3.at[ch, three], send_sem.at[2]).wait()
        return carry

    lax.fori_loop(0, CHUNKS, drain, 0)
    for n in range(1, 4):
        pltpu.make_async_copy(parts.at[n], parts.at[n], send_sem.at[2 + n]).wait()


def per_device(base_cells, offsets, charges, bias_coupling, counts, green):
    vmem = pl.BlockSpec(memory_space=pltpu.VMEM)
    hbm = pl.BlockSpec(memory_space=pltpu.HBM)
    potential, gradient = pl.pallas_call(
        main_kernel,
        out_shape=(
            jax.ShapeDtypeStruct((XD, ROWS, NZ), F32),
            jax.ShapeDtypeStruct((1, ATOMS), F32),
        ),
        in_specs=[pl.BlockSpec(memory_space=pltpu.SMEM)] + [vmem] * 3 + [hbm] * 2,
        out_specs=(hbm, vmem),
        scratch_shapes=[
            pltpu.VMEM((KY, C // 2, NX), F32),
            pltpu.VMEM((2, NZ, NZ), BF16),
            pltpu.VMEM((2, NX, 2 * NX), BF16),
            pltpu.VMEM((2, NX, 2 * NX), BF16),
            pltpu.VMEM((2, NX, 2 * NX), BF16),
            pltpu.VMEM((C, 256), BF16),
            pltpu.VMEM((8, ATOMS), F32),
            pltpu.VMEM((2, 2, N_DOM, 8, ATOMS), F32),
            pltpu.VMEM((KY, NX, C), F32),
            pltpu.VMEM((2, NX, 2 * NX), BF16),
            pltpu.VMEM((4, 2, NZ, ATOMS), BF16),
            pltpu.VMEM((2, ROWS + 8, ATOMS), F32),
            pltpu.VMEM((4, 8, ATOMS), F32),
            pltpu.VMEM((2, NY // 2, XD * C), F32),
            pltpu.VMEM((2, NY // 2, XD * C), F32),
            pltpu.VMEM((FAR, 2, XD, KY, C), F32),
            pltpu.VMEM((N_SLAB, XD, KY, C), F32),
            pltpu.VMEM((2, 2 * NX, KY * C), BF16),
            pltpu.VMEM((CHUNKS, N_SLAB, CHUNK, KY, C), F32),
            pltpu.VMEM((CHUNKS, N_SLAB, CHUNK, KY, C), F32),
            pltpu.VMEM((CHUNKS, N_DOM, CHUNK, ROWS, C), F32),
            pltpu.VMEM((CHUNKS, N_DOM, CHUNK, ROWS, C), F32),
            pltpu.VMEM((XD, ROWS, NZ), F32),
            pltpu.VMEM((4, 1, ATOMS), F32),
            pltpu.VMEM((4, 8, ATOMS), F32),
            pltpu.VMEM((4, 8, ATOMS), F32),
            pltpu.SemaphoreType.DMA((6,)),
            pltpu.SemaphoreType.DMA,
            pltpu.SemaphoreType.DMA((6,)),
            pltpu.SemaphoreType.DMA,
            pltpu.SemaphoreType.DMA((2, 2, N_DOM)),
            pltpu.SemaphoreType.DMA,
            pltpu.SemaphoreType.DMA((CHUNKS,)),
            pltpu.SemaphoreType.DMA((CHUNKS,)),
            pltpu.SemaphoreType.DMA((4,)),
        ],
        compiler_params=pltpu.CompilerParams(
            collective_id=1, has_side_effects=True, vmem_limit_bytes=64_500_000
        ),
        name="mesh",
    )(
        counts,
        base_cells,
        offsets,
        charges.reshape(1, ATOMS),
        green.transpose(1, 2, 0),
        jnp.asarray(constants()),
    )
    norm = 1.0 / (NX * NY * NZ)
    alive = jnp.arange(ATOMS, dtype=jnp.int32) < counts[0]
    gradient = jnp.where(alive, bias_coupling * (gradient.reshape(ATOMS) * norm), 0.0)
    return (potential * norm, gradient)


def solution(mesh):
    placed = (
        P(None, ("slab", "dom")),
        P(None, ("slab", "dom")),
        P(("slab", "dom")),
        P(("slab", "dom")),
        P(("slab", "dom")),
        P(None, "slab", "dom"),
    )
    return jax.shard_map(
        per_device,
        mesh=mesh,
        in_specs=placed,
        out_specs=(P("slab", "dom", None), P(("slab", "dom"))),
        check_vma=False,
    )
```

```python
import functools

import numpy as np
import jax
import jax.numpy as jnp
from jax import lax
from jax.experimental import pallas as pl
from jax.experimental.pallas import tpu as pltpu
from jax.sharding import PartitionSpec as P

XD = 4
NY = 512
NZ = 512
NX = 256
N_SLAB = 64
N_DOM = 4
ROWS = NY // N_DOM
KY = NY // N_SLAB
ATOMS = 256
C = 128
MESH = pl.DeviceIdType.MESH
F32 = jnp.float32
BF16 = jnp.bfloat16
CHUNK = 1
CHUNKS = XD // CHUNK
EXTRA = 16


def halves(table):
    table = np.asarray(table, np.float32)
    high = table.astype(jnp.bfloat16)
    low = (table - high.astype(np.float32)).astype(jnp.bfloat16)
    return np.stack([high, low])


def constants():
    kz_local = NZ // 2 // N_DOM
    kz = np.arange(NZ // 2)
    angle = 2 * np.pi * ((kz[:, None] * np.arange(NZ)[None, :]) % NZ) / NZ
    fz = np.stack([np.cos(angle).reshape(N_DOM, kz_local, NZ), -np.sin(angle).reshape(N_DOM, kz_local, NZ)], 1)
    fz = fz.reshape(2 * kz_local * N_DOM, NZ)
    k = np.arange(256)
    even = 2 * np.pi * ((k[:, None] * k[None, :]) % 256) / 256
    odd = 2 * np.pi * ((k[:, None] * (2 * k[None, :] + 1)) % 512) / 512
    cs_even = np.concatenate([np.cos(even), np.sin(even)], 1)
    cs_odd = np.concatenate([np.cos(odd), np.sin(odd)], 1)
    cs_odd_t = np.concatenate([np.cos(odd).T, np.sin(odd).T], 1)
    main = halves(np.concatenate([fz, cs_even, cs_odd, cs_odd_t], 0))
    coarse, fine = halves(fz[:, ::16]), halves(fz[:, :32])
    blank = np.zeros((NZ, 64), jnp.bfloat16)
    pair = np.concatenate([coarse[0], coarse[1], blank, fine[0], fine[0], fine[1], blank[:, :32]], 1)
    pair = pair.reshape(2, 2, C, 256).transpose(0, 2, 1, 3).reshape(2, C, 512)
    return np.concatenate([main, pair], 1)


def split(value):
    high = value.astype(BF16)
    low = (value - high.astype(F32)).astype(BF16)
    return high, low


NN = (((1,), (0,)), ((), ()))
NT = (((1,), (1,)), ((), ()))


def dot3(a, b, dims=NN):
    def dot(x, y):
        return lax.dot_general(x, y, dims, preferred_element_type=F32)

    return dot(a[0], b[0]) + (dot(a[0], b[1]) + dot(a[1], b[0]))


def spline_rows(frac):
    inner = 1.0 - frac
    square = frac * frac
    cube = square * frac
    return [
        inner * inner * inner * (1.0 / 6.0),
        (3.0 * cube - 6.0 * square + 4.0) * (1.0 / 6.0),
        (-3.0 * cube + 3.0 * square + 3.0 * frac + 1.0) * (1.0 / 6.0),
        cube * (1.0 / 6.0),
    ]


def hot(t, weights):
    out = jnp.where(t == 0, weights[0], 0.0)
    for step in range(1, 4):
        out = jnp.where(t == step, weights[step], out)
    return out


def turned(value, sign):
    lane = lax.broadcasted_iota(jnp.int32, (1, C), 1)
    factor = jnp.where(lane < C // 2, sign, -sign).astype(F32)
    parts = [pltpu.roll(value[:, i : i + C], C // 2, 1) * factor for i in range(0, value.shape[1], C)]
    return jnp.concatenate(parts, 1)


def stacked(value, sign):
    return split(jnp.concatenate([value, turned(value, sign)], 0))


def shifted_slab(s, k):
    z, y, c = s // 8, (s // 2) % 4, s % 2
    dz, dy, dc = k // 8, (k // 2) % 4, k % 2
    return ((z + dz) % 8) * 8 + ((y + dy) % 4) * 2 + (c + dc) % 2


FAR = N_SLAB // 2
SENDS = ((0, 0, 0), (0, 1, 1), (1, 0, FAR), (1, 1, FAR + 1))
AWAY = (0, 1, N_SLAB - 1, FAR, FAR + 1, FAR - 1)


def near_plane(z, m):
    first = z + 7 - z % 2
    return (first + (m + 64 - first) % 4) % 8


def signal(target):
    pl.semaphore_signal(pltpu.get_barrier_semaphore(), inc=1, device_id=target, device_id_type=MESH)


def main_kernel(
    counts_ref, cells_ref, offsets_ref, charges_ref, green_hbm, table_hbm,
    pot_hbm, grad_ref,
    green, fz, even_m, odd_m, back_odd, phases,
    own_ref, atoms_ref, factors, by_plane,
    hot_z, wy_tab, wx_tab, grid_even, grid_odd, send1, recv1, spectrum, send2, recv2, send3, recv3,
    pot_ref, totals, parts, parts_in,
    load_sem, pot_sem, send_sem, atom_send, atom_recv, r1, r2, r3, r4,
):
    s, d = lax.axis_index("slab"), lax.axis_index("dom")
    nxt, prv = (s + 1) % N_SLAB, (s + N_SLAB - 1) % N_SLAB
    right, left = (d + 1) % N_DOM, (d + N_DOM - 1) % N_DOM

    def greet(k, carry):
        signal((shifted_slab(s, k), d))
        return carry

    for i in range(1, N_DOM):
        for step in AWAY:
            signal(((s + step) % N_SLAB, (d + i) % N_DOM))
    lax.fori_loop(1, N_SLAB, greet, 0)

    loads = [
        pltpu.make_async_copy(src, dst, load_sem.at[i])
        for i, (src, dst) in enumerate(
            [
                (table_hbm.at[:, 0:NZ], fz),
                (table_hbm.at[:, NZ : NZ + NX], even_m),
                (table_hbm.at[:, NZ + NX : NZ + 2 * NX], odd_m),
                (green_hbm, green),
                (table_hbm.at[:, NZ + 2 * NX : NZ + 3 * NX], back_odd),
                (
                    table_hbm.at[d // 2, pl.ds(NZ + 3 * NX, C), pl.ds(pl.multiple_of((d % 2) * 256, 256), 256)],
                    phases,
                ),
            ]
        )
    ]
    for load in loads:
        load.start()

    slot = lax.broadcasted_iota(jnp.int32, (1, ATOMS), 1)
    alive = slot < counts_ref[...]
    own_ref[0:1] = (cells_ref[0:1] % XD).astype(F32)
    own_ref[1:2] = (cells_ref[1:2] % ROWS).astype(F32)
    own_ref[2:3] = cells_ref[2:3].astype(F32)
    own_ref[3:6] = offsets_ref[...]
    own_ref[6:7] = jnp.where(alive, charges_ref[...], 0.0)
    own_ref[7:8] = jnp.zeros((1, ATOMS), F32)
    atoms_ref[0, 0, d] = own_ref[...]
    grid_even[...] = jnp.zeros_like(grid_even)
    grid_odd[...] = jnp.zeros_like(grid_odd)
    totals[...] = jnp.zeros_like(totals)

    loads[1].wait()
    r = lax.broadcasted_iota(jnp.int32, (NX, NX), 0)
    x = lax.broadcasted_iota(jnp.int32, (NX, NX), 1)
    per = N_SLAB * CHUNK
    chosen = XD * ((r % per) // CHUNK) + CHUNK * (r // per) + r % CHUNK
    pick = jnp.where(x == chosen, 1.0, 0.0).astype(BF16)
    for n in range(2):
        by_plane[n] = lax.dot_general(pick, even_m[n], NN, preferred_element_type=F32).astype(BF16)

    loads[3].wait()
    lane = lax.broadcasted_iota(jnp.int32, (1, C), 1)
    zero_bin = jnp.logical_and(lane % (C // 2) == 0, d == 0)
    scale = jnp.where(zero_bin, 1.0, 2.0).astype(F32)

    def prepare(t, carry):
        f = green[t]
        factors[t] = jnp.concatenate([f, f], 0).T * scale
        return carry

    lax.fori_loop(0, KY, prepare, 0)

    pl.semaphore_wait(pltpu.get_barrier_semaphore(), N_SLAB - 1 + len(AWAY) * (N_DOM - 1))

    for h, g, step in SENDS:
        for i in range(N_DOM):
            if h == g == i == 0:
                continue
            pltpu.make_async_remote_copy(
                own_ref,
                atoms_ref.at[h, g, d],
                atom_send,
                atom_recv.at[h, g, i],
                device_id=((s + step) % N_SLAB, (d + i) % N_DOM),
                device_id_type=MESH,
            ).start()

    row_h = lax.broadcasted_iota(jnp.int32, (64, ATOMS), 0) % 32
    row_l = lax.broadcasted_iota(jnp.int32, (32, ATOMS), 0)
    row = lax.broadcasted_iota(jnp.int32, (ROWS + EXTRA, ATOMS), 0)
    half = ROWS // 2
    row_y = jnp.where(
        row < ROWS,
        2 * (row % half) + row // half,
        ROWS + 2 * ((row - ROWS) % (EXTRA // 2)) + (row - ROWS) // (EXTRA // 2),
    )
    row_x = lax.broadcasted_iota(jnp.int32, (8, ATOMS), 0)
    loads[5].wait()

    z, inner = s // 8, s % 8
    served = near_plane(z, lax.broadcasted_iota(jnp.int32, (NX, 2 * C), 0) // 64)
    sign = jnp.where(served < 4, 1.0, -1.0).astype(F32)
    here = (z % 4) * 8 + inner
    loads[2].wait()

    def spread(i, h):
        e = (d + i) % N_DOM
        rows_y, scaled = [], []
        for g in range(2):

            def arrive():
                block = atoms_ref.at[h, g, e]
                pltpu.make_async_copy(block, block, atom_recv.at[h, g, (N_DOM - i) % N_DOM]).wait()

            if g == 0:
                pl.when(h + i > 0)(arrive)
            else:
                arrive()
            data = atoms_ref[h, g, e]
            whole = data[0:3].astype(jnp.int32)
            cell = whole[2:3]
            coarse = jnp.where(row_h == cell // 16, 1.0, 0.0).astype(BF16)
            fine = split(hot(row_l - cell % 16, spline_rows(data[5:6])))
            a = jnp.dot(phases[:, :64], coarse, preferred_element_type=F32)
            b = jnp.dot(
                phases[:, C : C + 96],
                jnp.concatenate([fine[0], fine[1], fine[0]], 0),
                preferred_element_type=F32,
            )
            a_re, a_im, b_re, b_im = a[: C // 2], a[C // 2 :], b[: C // 2], b[C // 2 :]
            lines = jnp.concatenate([a_re * b_re - a_im * b_im, a_re * b_im + a_im * b_re], 0) * data[6:7]
            wx = hot(row_x - whole[0:1] + XD * g, spline_rows(data[3:4]))
            rows_y.append(hot(row_y - whole[1:2], spline_rows(data[4:5])))
            scaled.append(jnp.concatenate([lines * wx[p : p + 1] for p in range(XD)], 0))
        out = dot3(split(jnp.concatenate(rows_y, 1)), split(jnp.concatenate(scaled, 1)), NT)
        own_rows = pl.ds(pl.multiple_of(e * half, half), half)
        after = pl.ds(pl.multiple_of(((e + 1) % N_DOM) * half, half), EXTRA // 2)
        grid_even[h, own_rows, :] += out[:half]
        grid_odd[h, own_rows, :] += out[half:ROWS]
        grid_even[h, after, :] += out[ROWS : ROWS + EXTRA // 2]
        grid_odd[h, after, :] += out[ROWS + EXTRA // 2 :]
        return h

    def outward(h, carry):
        lax.fori_loop(0, N_DOM, spread, h)
        for pair in range(2):
            lanes = slice(2 * C * pair, 2 * C * (pair + 1))
            a = dot3((even_m[0], even_m[1]), stacked(grid_even[h, :, lanes], 1.0))
            b = dot3((odd_m[0], odd_m[1]), stacked(grid_odd[h, :, lanes], 1.0))
            value = a + sign * b
            for q in range(2):
                send1[:, h, 2 * pair + q] = value[:, C * q : C * (q + 1)].reshape(FAR, KY, C)

        def post1(k, inside):
            j = (here + 13 * k) % FAR
            t = near_plane(z, j // 8) * 8 + j % 8
            pltpu.make_async_remote_copy(
                send1.at[j, h],
                recv1.at[(s + FAR * h) % N_SLAB],
                send_sem.at[0],
                r1,
                device_id=(t, d),
                device_id_type=MESH,
            ).start()
            return inside

        lax.fori_loop(1, FAR, post1, 0)
        return carry

    lax.fori_loop(0, 2, outward, 0)
    for h in range(2):
        recv1[(s + FAR * h) % N_SLAB] = send1[here, h]
    natural = lax.broadcasted_iota(jnp.int32, (ROWS, ATOMS), 0)
    row_z = lax.broadcasted_iota(jnp.int32, (NZ, ATOMS), 0)
    for g in range(2):
        for n, first, size, e in ((0, 0, ROWS, d), (1, ROWS, 8, left)):
            data = atoms_ref[0, g, e]
            whole = data[0:3].astype(jnp.int32)
            wy_tab[g, first : first + size] = hot(first + natural[:size] - whole[1:2], spline_rows(data[4:5]))
            wx_tab[2 * n + g] = hot(row_x - whole[0:1] + XD * g, spline_rows(data[3:4]))
            hz = split(hot((row_z - whole[2:3]) & (NZ - 1), spline_rows(data[5:6])))
            hot_z[2 * n + g, 0] = hz[0]
            hot_z[2 * n + g, 1] = hz[1]
    others = pl.ds(0, N_SLAB - 1)
    sent1 = pl.ds(0, N_SLAB - 2)
    pltpu.make_async_copy(recv1.at[sent1], recv1.at[sent1], r1).wait()

    flat1 = recv1.reshape(NX * KY, C)
    for pair in range(KY // 2):
        value = jnp.concatenate([flat1[pl.ds(2 * pair + q, NX, stride=KY), :] for q in range(2)], 1)
        spec = dot3((even_m[0], even_m[1]), stacked(value, 1.0))
        spec = spec * jnp.concatenate([factors[2 * pair], factors[2 * pair + 1]], 1)
        high, low = stacked(spec, -1.0)
        spectrum[0, :, 2 * C * pair : 2 * C * (pair + 1)] = high
        spectrum[1, :, 2 * C * pair : 2 * C * (pair + 1)] = low

    flat2 = send2.reshape(CHUNKS, per * KY, C)

    def along_x(ch, carry):
        rows = pl.ds(pl.multiple_of(ch * per, per), per)
        out = dot3((by_plane[0, rows], by_plane[1, rows]), (spectrum[0], spectrum[1]))
        for t in range(KY):
            flat2[ch, pl.ds(t, per, stride=KY), :] = out[:, C * t : C * (t + 1)]

        def post2(k, inner):
            t = shifted_slab(s, (29 * k) % N_SLAB)
            pltpu.make_async_remote_copy(
                send2.at[ch, t],
                recv2.at[ch, s],
                send_sem.at[1],
                r2.at[ch],
                device_id=(t, d),
                device_id_type=MESH,
            ).start()
            return inner

        lax.fori_loop(1, N_SLAB, post2, 0)
        recv2[ch, s] = send2[ch, s]
        return carry

    lax.fori_loop(0, CHUNKS, along_x, 0)
    loads[0].wait()
    loads[4].wait()
    three = pl.ds(0, N_DOM - 1)

    def deliver(n):
        target = ((s, left), (prv, d), (prv, left))[n - 1]
        parts[n] = jnp.broadcast_to(totals[n], (8, ATOMS))
        pltpu.make_async_remote_copy(
            parts.at[n], parts_in.at[n], send_sem.at[2 + n], r4.at[n], device_id=target, device_id_type=MESH
        ).start()

    def finish(ch, carry):
        @pl.when(ch < CHUNKS)
        def _():
            pltpu.make_async_copy(recv2.at[ch, others], recv2.at[ch, others], r2.at[ch]).wait()
            value = jnp.concatenate([recv2[ch, :, q].reshape(NY, C) for q in range(CHUNK)], 1)
            low, high = value[: NY // 2], value[NY // 2 :]
            even = dot3((even_m[0], even_m[1]), stacked(low + high, -1.0))
            odd = dot3((back_odd[0], back_odd[1]), stacked(low - high, -1.0))
            for q in range(CHUNK):
                lanes = slice(C * q, C * (q + 1))
                for e in range(N_DOM):
                    send3[ch, e, q, pl.ds(0, half, stride=2), :] = even[e * half : (e + 1) * half, lanes]
                    send3[ch, e, q, pl.ds(1, half, stride=2), :] = odd[e * half : (e + 1) * half, lanes]
            for i in range(1, N_DOM):
                e = (d + i) % N_DOM
                pltpu.make_async_remote_copy(
                    send3.at[ch, e],
                    recv3.at[ch, d],
                    send_sem.at[2],
                    r3.at[ch],
                    device_id=(s, e),
                    device_id_type=MESH,
                ).start()
            recv3[ch, d] = send3[ch, d]

        @pl.when(ch > 0)
        def _():
            c = ch - 1
            pltpu.make_async_copy(recv3.at[c, three], recv3.at[c, three], r3.at[c]).wait()
            columns = jnp.concatenate([recv3[c, e].reshape(CHUNK * ROWS, C) for e in range(N_DOM)], 1)
            block = dot3(split(columns), (fz[0], fz[1]))
            for q in range(CHUNK):
                pot_ref[CHUNK * c + q] = block[q * ROWS : (q + 1) * ROWS]
            done = pl.ds(pl.multiple_of(CHUNK * c, CHUNK), CHUNK)
            pltpu.make_async_copy(pot_ref.at[done], pot_hbm.at[done], pot_sem).start()
            both = split(block)
            edge = split(jnp.concatenate([block[q * ROWS : q * ROWS + 8] for q in range(CHUNK)], 0))

            def sample(g):
                u = dot3(both, (hot_z[g, 0], hot_z[g, 1]))
                v = dot3(edge, (hot_z[2 + g, 0], hot_z[2 + g, 1]))
                for q in range(CHUNK):
                    p = CHUNK * c + q
                    here = jnp.sum(u[q * ROWS : (q + 1) * ROWS] * wy_tab[g, :ROWS], 0, keepdims=True)
                    there = jnp.sum(v[q * 8 : (q + 1) * 8] * wy_tab[g, ROWS:], 0, keepdims=True)
                    totals[2 * g] += here * wx_tab[g, pl.ds(p, 1)]
                    totals[2 * g + 1] += there * wx_tab[2 + g, pl.ds(p, 1)]

            sample(0)

            @pl.when(c < CHUNKS - 1)
            def _():
                sample(1)

            @pl.when(c == CHUNKS - 2)
            def _():
                deliver(2)
                deliver(3)

        return carry

    lax.fori_loop(0, CHUNKS + 1, finish, 0)

    deliver(1)
    for n in range(1, 4):
        pltpu.make_async_copy(parts_in.at[n], parts_in.at[n], r4.at[n]).wait()
    total = totals[0] + parts_in[1, 0:1] + parts_in[2, 0:1] + parts_in[3, 0:1]
    grad_ref[...] = total * (1.0 / (NX * NY * NZ))
    pltpu.make_async_copy(pot_ref, pot_hbm, pot_sem).wait()

    gone = atoms_ref.reshape(4 * N_DOM, 8, ATOMS).at[pl.ds(0, 4 * N_DOM - 1)]
    pltpu.make_async_copy(gone, gone, atom_send).wait()
    pltpu.make_async_copy(recv1.at[sent1], recv1.at[sent1], send_sem.at[0]).wait()

    def drain(ch, carry):
        pltpu.make_async_copy(send2.at[ch, others], send2.at[ch, others], send_sem.at[1]).wait()
        pltpu.make_async_copy(send3.at[ch, three], send3.at[ch, three], send_sem.at[2]).wait()
        return carry

    lax.fori_loop(0, CHUNKS, drain, 0)
    for n in range(1, 4):
        pltpu.make_async_copy(parts.at[n], parts.at[n], send_sem.at[2 + n]).wait()


def per_device(base_cells, offsets, charges, bias_coupling, counts, green):
    vmem = pl.BlockSpec(memory_space=pltpu.VMEM)
    hbm = pl.BlockSpec(memory_space=pltpu.HBM)
    potential, gradient = pl.pallas_call(
        main_kernel,
        out_shape=(
            jax.ShapeDtypeStruct((XD, ROWS, NZ), F32),
            jax.ShapeDtypeStruct((1, ATOMS), F32),
        ),
        in_specs=[vmem] * 4 + [hbm] * 2,
        out_specs=(hbm, vmem),
        scratch_shapes=[
            pltpu.VMEM((KY, C // 2, NX), F32),
            pltpu.VMEM((2, NZ, NZ), BF16),
            pltpu.VMEM((2, NX, 2 * NX), BF16),
            pltpu.VMEM((2, NX, 2 * NX), BF16),
            pltpu.VMEM((2, NX, 2 * NX), BF16),
            pltpu.VMEM((C, 256), BF16),
            pltpu.VMEM((8, ATOMS), F32),
            pltpu.VMEM((2, 2, N_DOM, 8, ATOMS), F32),
            pltpu.VMEM((KY, NX, C), F32),
            pltpu.VMEM((2, NX, 2 * NX), BF16),
            pltpu.VMEM((4, 2, NZ, ATOMS), BF16),
            pltpu.VMEM((2, ROWS + 8, ATOMS), F32),
            pltpu.VMEM((4, 8, ATOMS), F32),
            pltpu.VMEM((2, NY // 2, XD * C), F32),
            pltpu.VMEM((2, NY // 2, XD * C), F32),
            pltpu.VMEM((FAR, 2, XD, KY, C), F32),
            pltpu.VMEM((N_SLAB, XD, KY, C), F32),
            pltpu.VMEM((2, 2 * NX, KY * C), BF16),
            pltpu.VMEM((CHUNKS, N_SLAB, CHUNK, KY, C), F32),
            pltpu.VMEM((CHUNKS, N_SLAB, CHUNK, KY, C), F32),
            pltpu.VMEM((CHUNKS, N_DOM, CHUNK, ROWS, C), F32),
            pltpu.VMEM((CHUNKS, N_DOM, CHUNK, ROWS, C), F32),
            pltpu.VMEM((XD, ROWS, NZ), F32),
            pltpu.VMEM((4, 1, ATOMS), F32),
            pltpu.VMEM((4, 8, ATOMS), F32),
            pltpu.VMEM((4, 8, ATOMS), F32),
            pltpu.SemaphoreType.DMA((6,)),
            pltpu.SemaphoreType.DMA,
            pltpu.SemaphoreType.DMA((6,)),
            pltpu.SemaphoreType.DMA,
            pltpu.SemaphoreType.DMA((2, 2, N_DOM)),
            pltpu.SemaphoreType.DMA,
            pltpu.SemaphoreType.DMA((CHUNKS,)),
            pltpu.SemaphoreType.DMA((CHUNKS,)),
            pltpu.SemaphoreType.DMA((4,)),
        ],
        compiler_params=pltpu.CompilerParams(
            collective_id=1, has_side_effects=True, vmem_limit_bytes=64_500_000
        ),
        name="mesh",
    )(
        counts.reshape(1, 1),
        base_cells,
        offsets,
        charges.reshape(1, ATOMS),
        green.transpose(1, 2, 0),
        jnp.asarray(constants()),
    )
    norm = 1.0 / (NX * NY * NZ)
    alive = jnp.arange(ATOMS, dtype=jnp.int32) < counts[0]
    gradient = jnp.where(alive, bias_coupling * gradient.reshape(ATOMS), 0.0)
    return (potential * norm, gradient)


def solution(mesh):
    placed = (
        P(None, ("slab", "dom")),
        P(None, ("slab", "dom")),
        P(("slab", "dom")),
        P(("slab", "dom")),
        P(("slab", "dom")),
        P(None, "slab", "dom"),
    )
    return jax.shard_map(
        per_device,
        mesh=mesh,
        in_specs=placed,
        out_specs=(P("slab", "dom", None), P(("slab", "dom"))),
        check_vma=False,
    )
```

```python
import functools

import numpy as np
import jax
import jax.numpy as jnp
from jax import lax
from jax.experimental import pallas as pl
from jax.experimental.pallas import tpu as pltpu
from jax.sharding import PartitionSpec as P

XD = 4
NY = 512
NZ = 512
NX = 256
N_SLAB = 64
N_DOM = 4
ROWS = NY // N_DOM
KY = NY // N_SLAB
ATOMS = 256
C = 128
MESH = pl.DeviceIdType.MESH
F32 = jnp.float32
BF16 = jnp.bfloat16
CHUNK = 1
CHUNKS = XD // CHUNK
EXTRA = 16


def halves(table):
    table = np.asarray(table, np.float32)
    high = table.astype(jnp.bfloat16)
    low = (table - high.astype(np.float32)).astype(jnp.bfloat16)
    return np.stack([high, low])


def constants():
    kz_local = NZ // 2 // N_DOM
    kz = np.arange(NZ // 2)
    angle = 2 * np.pi * ((kz[:, None] * np.arange(NZ)[None, :]) % NZ) / NZ
    fz = np.stack([np.cos(angle).reshape(N_DOM, kz_local, NZ), -np.sin(angle).reshape(N_DOM, kz_local, NZ)], 1)
    fz = fz.reshape(2 * kz_local * N_DOM, NZ)
    k = np.arange(256)
    even = 2 * np.pi * ((k[:, None] * k[None, :]) % 256) / 256
    odd = 2 * np.pi * ((k[:, None] * (2 * k[None, :] + 1)) % 512) / 512
    cs_even = np.concatenate([np.cos(even), np.sin(even)], 1)
    cs_odd = np.concatenate([np.cos(odd), np.sin(odd)], 1)
    cs_odd_t = np.concatenate([np.cos(odd).T, np.sin(odd).T], 1)
    main = halves(np.concatenate([fz, cs_even, cs_odd, cs_odd_t], 0))
    coarse, fine = halves(fz[:, ::16]), halves(fz[:, :32])
    blank = np.zeros((NZ, 64), jnp.bfloat16)
    pair = np.concatenate([coarse[0], coarse[1], blank, fine[0], fine[0], fine[1], blank[:, :32]], 1)
    pair = pair.reshape(2, 2, C, 256).transpose(0, 2, 1, 3).reshape(2, C, 512)
    return np.concatenate([main, pair], 1)


def split(value):
    high = value.astype(BF16)
    low = (value - high.astype(F32)).astype(BF16)
    return high, low


NN = (((1,), (0,)), ((), ()))
NT = (((1,), (1,)), ((), ()))


def dot3(a, b, dims=NN):
    def dot(x, y):
        return lax.dot_general(x, y, dims, preferred_element_type=F32)

    return dot(a[0], b[0]) + (dot(a[0], b[1]) + dot(a[1], b[0]))


def spline_rows(frac):
    inner = 1.0 - frac
    square = frac * frac
    cube = square * frac
    return [
        inner * inner * inner * (1.0 / 6.0),
        (3.0 * cube - 6.0 * square + 4.0) * (1.0 / 6.0),
        (-3.0 * cube + 3.0 * square + 3.0 * frac + 1.0) * (1.0 / 6.0),
        cube * (1.0 / 6.0),
    ]


def hot(t, weights):
    out = jnp.where(t == 0, weights[0], 0.0)
    for step in range(1, 4):
        out = jnp.where(t == step, weights[step], out)
    return out


def turned(value, sign):
    lane = lax.broadcasted_iota(jnp.int32, (1, C), 1)
    factor = jnp.where(lane < C // 2, sign, -sign).astype(F32)
    parts = [pltpu.roll(value[:, i : i + C], C // 2, 1) * factor for i in range(0, value.shape[1], C)]
    return jnp.concatenate(parts, 1)


def stacked(value, sign):
    return split(jnp.concatenate([value, turned(value, sign)], 0))


def shifted_slab(s, k):
    z, y, c = s // 8, (s // 2) % 4, s % 2
    dz, dy, dc = k // 8, (k // 2) % 4, k % 2
    return ((z + dz) % 8) * 8 + ((y + dy) % 4) * 2 + (c + dc) % 2


FAR = N_SLAB // 2
SENDS = ((0, 0, 0), (0, 1, 1), (1, 0, FAR), (1, 1, FAR + 1))
AWAY = (0, 1, N_SLAB - 1, FAR, FAR + 1, FAR - 1)


def near_plane(z, m):
    first = z + 7 - z % 2
    return (first + (m + 64 - first) % 4) % 8


def signal(target):
    pl.semaphore_signal(pltpu.get_barrier_semaphore(), inc=1, device_id=target, device_id_type=MESH)


def main_kernel(
    counts_ref, cells_ref, offsets_ref, charges_ref, green_hbm, table_hbm,
    pot_hbm, grad_ref,
    green, fz, even_m, odd_m, back_odd, phases,
    own_ref, atoms_ref, factors, by_plane,
    hot_z, wy_tab, wx_tab, grid_even, grid_odd, send1, recv1, spectrum, send2, recv2, send3, recv3,
    pot_ref, totals, parts, parts_in,
    load_sem, pot_sem, send_sem, atom_send, atom_recv, r1, r2, r3, r4,
):
    s, d = lax.axis_index("slab"), lax.axis_index("dom")
    nxt, prv = (s + 1) % N_SLAB, (s + N_SLAB - 1) % N_SLAB
    right, left = (d + 1) % N_DOM, (d + N_DOM - 1) % N_DOM

    def greet(k, carry):
        signal((shifted_slab(s, k), d))
        return carry

    for i in range(1, N_DOM):
        for step in AWAY:
            signal(((s + step) % N_SLAB, (d + i) % N_DOM))
    lax.fori_loop(1, N_SLAB, greet, 0)

    loads = [
        pltpu.make_async_copy(src, dst, load_sem.at[i])
        for i, (src, dst) in enumerate(
            [
                (table_hbm.at[:, 0:NZ], fz),
                (table_hbm.at[:, NZ : NZ + NX], even_m),
                (table_hbm.at[:, NZ + NX : NZ + 2 * NX], odd_m),
                (green_hbm, green),
                (table_hbm.at[:, NZ + 2 * NX : NZ + 3 * NX], back_odd),
                (
                    table_hbm.at[d // 2, pl.ds(NZ + 3 * NX, C), pl.ds(pl.multiple_of((d % 2) * 256, 256), 256)],
                    phases,
                ),
            ]
        )
    ]
    for load in loads:
        load.start()

    slot = lax.broadcasted_iota(jnp.int32, (1, ATOMS), 1)
    alive = slot < counts_ref[...]
    own_ref[0:1] = (cells_ref[0:1] % XD).astype(F32)
    own_ref[1:2] = (cells_ref[1:2] % ROWS).astype(F32)
    own_ref[2:3] = cells_ref[2:3].astype(F32)
    own_ref[3:6] = offsets_ref[...]
    own_ref[6:7] = jnp.where(alive, charges_ref[...], 0.0)
    own_ref[7:8] = jnp.zeros((1, ATOMS), F32)
    atoms_ref[0, 0, d] = own_ref[...]
    grid_even[...] = jnp.zeros_like(grid_even)
    grid_odd[...] = jnp.zeros_like(grid_odd)
    totals[...] = jnp.zeros_like(totals)

    loads[1].wait()
    r = lax.broadcasted_iota(jnp.int32, (NX, NX), 0)
    x = lax.broadcasted_iota(jnp.int32, (NX, NX), 1)
    per = N_SLAB * CHUNK
    chosen = XD * ((r % per) // CHUNK) + CHUNK * (r // per) + r % CHUNK
    pick = jnp.where(x == chosen, 1.0, 0.0).astype(BF16)
    for n in range(2):
        by_plane[n] = lax.dot_general(pick, even_m[n], NN, preferred_element_type=F32).astype(BF16)

    loads[3].wait()
    lane = lax.broadcasted_iota(jnp.int32, (1, C), 1)
    zero_bin = jnp.logical_and(lane % (C // 2) == 0, d == 0)
    scale = jnp.where(zero_bin, 1.0, 2.0).astype(F32)

    def prepare(t, carry):
        f = green[t]
        factors[t] = jnp.concatenate([f, f], 0).T * scale
        return carry

    lax.fori_loop(0, KY, prepare, 0)

    pl.semaphore_wait(pltpu.get_barrier_semaphore(), N_SLAB - 1 + len(AWAY) * (N_DOM - 1))

    for h, g, step in SENDS:
        for i in range(N_DOM):
            if h == g == i == 0:
                continue
            pltpu.make_async_remote_copy(
                own_ref,
                atoms_ref.at[h, g, d],
                atom_send,
                atom_recv.at[h, g, i],
                device_id=((s + step) % N_SLAB, (d + i) % N_DOM),
                device_id_type=MESH,
            ).start()

    row_h = lax.broadcasted_iota(jnp.int32, (64, ATOMS), 0) % 32
    row_l = lax.broadcasted_iota(jnp.int32, (32, ATOMS), 0)
    row = lax.broadcasted_iota(jnp.int32, (ROWS + EXTRA, ATOMS), 0)
    half = ROWS // 2
    row_y = jnp.where(
        row < ROWS,
        2 * (row % half) + row // half,
        ROWS + 2 * ((row - ROWS) % (EXTRA // 2)) + (row - ROWS) // (EXTRA // 2),
    )
    row_x = lax.broadcasted_iota(jnp.int32, (8, ATOMS), 0)
    loads[5].wait()

    z, inner = s // 8, s % 8
    served = near_plane(z, lax.broadcasted_iota(jnp.int32, (NX, 2 * C), 0) // 64)
    sign = jnp.where(served < 4, 1.0, -1.0).astype(F32)
    here = (z % 4) * 8 + inner
    loads[2].wait()

    def spread(i, h):
        e = (d + i) % N_DOM
        rows_y, scaled = [], []
        for g in range(2):

            def arrive():
                block = atoms_ref.at[h, g, e]
                pltpu.make_async_copy(block, block, atom_recv.at[h, g, (N_DOM - i) % N_DOM]).wait()

            if g == 0:
                pl.when(h + i > 0)(arrive)
            else:
                arrive()
            data = atoms_ref[h, g, e]
            whole = data[0:3].astype(jnp.int32)
            cell = whole[2:3]
            coarse = jnp.where(row_h == cell // 16, 1.0, 0.0).astype(BF16)
            fine = split(hot(row_l - cell % 16, spline_rows(data[5:6])))
            a = jnp.dot(phases[:, :64], coarse, preferred_element_type=F32)
            b = jnp.dot(
                phases[:, C : C + 96],
                jnp.concatenate([fine[0], fine[1], fine[0]], 0),
                preferred_element_type=F32,
            )
            a_re, a_im, b_re, b_im = a[: C // 2], a[C // 2 :], b[: C // 2], b[C // 2 :]
            lines = jnp.concatenate([a_re * b_re - a_im * b_im, a_re * b_im + a_im * b_re], 0) * data[6:7]
            wx = hot(row_x - whole[0:1] + XD * g, spline_rows(data[3:4]))
            rows_y.append(hot(row_y - whole[1:2], spline_rows(data[4:5])))
            scaled.append(jnp.concatenate([lines * wx[p : p + 1] for p in range(XD)], 0))
        out = dot3(split(jnp.concatenate(rows_y, 1)), split(jnp.concatenate(scaled, 1)), NT)
        own_rows = pl.ds(pl.multiple_of(e * half, half), half)
        after = pl.ds(pl.multiple_of(((e + 1) % N_DOM) * half, half), EXTRA // 2)
        grid_even[h, own_rows, :] += out[:half]
        grid_odd[h, own_rows, :] += out[half:ROWS]
        grid_even[h, after, :] += out[ROWS : ROWS + EXTRA // 2]
        grid_odd[h, after, :] += out[ROWS + EXTRA // 2 :]
        return h

    def outward(h, carry):
        lax.fori_loop(0, N_DOM, spread, h)
        for pair in range(2):
            lanes = slice(2 * C * pair, 2 * C * (pair + 1))
            a = dot3((even_m[0], even_m[1]), stacked(grid_even[h, :, lanes], 1.0))
            b = dot3((odd_m[0], odd_m[1]), stacked(grid_odd[h, :, lanes], 1.0))
            value = a + sign * b
            for q in range(2):
                send1[:, h, 2 * pair + q] = value[:, C * q : C * (q + 1)].reshape(FAR, KY, C)

        def post1(k, inside):
            j = (here + 13 * k) % FAR
            t = near_plane(z, j // 8) * 8 + j % 8
            pltpu.make_async_remote_copy(
                send1.at[j, h],
                recv1.at[(s + FAR * h) % N_SLAB],
                send_sem.at[0],
                r1,
                device_id=(t, d),
                device_id_type=MESH,
            ).start()
            return inside

        lax.fori_loop(1, FAR, post1, 0)
        return carry

    lax.fori_loop(0, 2, outward, 0)
    for h in range(2):
        recv1[(s + FAR * h) % N_SLAB] = send1[here, h]
    natural = lax.broadcasted_iota(jnp.int32, (ROWS, ATOMS), 0)
    row_z = lax.broadcasted_iota(jnp.int32, (NZ, ATOMS), 0)
    for g in range(2):
        for n, first, size, e in ((0, 0, ROWS, d), (1, ROWS, 8, left)):
            data = atoms_ref[0, g, e]
            whole = data[0:3].astype(jnp.int32)
            wy_tab[g, first : first + size] = hot(first + natural[:size] - whole[1:2], spline_rows(data[4:5]))
            wx_tab[2 * n + g] = hot(row_x - whole[0:1] + XD * g, spline_rows(data[3:4]))
            hz = split(hot((row_z - whole[2:3]) & (NZ - 1), spline_rows(data[5:6])))
            hot_z[2 * n + g, 0] = hz[0]
            hot_z[2 * n + g, 1] = hz[1]
    others = pl.ds(0, N_SLAB - 1)
    sent1 = pl.ds(0, N_SLAB - 2)
    pltpu.make_async_copy(recv1.at[sent1], recv1.at[sent1], r1).wait()

    flat1 = recv1.reshape(NX * KY, C)
    for pair in range(KY // 2):
        value = jnp.concatenate([flat1[pl.ds(2 * pair + q, NX, stride=KY), :] for q in range(2)], 1)
        spec = dot3((even_m[0], even_m[1]), stacked(value, 1.0))
        spec = spec * jnp.concatenate([factors[2 * pair], factors[2 * pair + 1]], 1)
        high, low = stacked(spec, -1.0)
        spectrum[0, :, 2 * C * pair : 2 * C * (pair + 1)] = high
        spectrum[1, :, 2 * C * pair : 2 * C * (pair + 1)] = low

    flat2 = send2.reshape(CHUNKS, per * KY, C)

    def along_x(ch, carry):
        rows = pl.ds(pl.multiple_of(ch * per, per), per)
        out = dot3((by_plane[0, rows], by_plane[1, rows]), (spectrum[0], spectrum[1]))
        for t in range(KY):
            flat2[ch, pl.ds(t, per, stride=KY), :] = out[:, C * t : C * (t + 1)]

        def post2(k, inner):
            t = shifted_slab(s, (29 * k) % N_SLAB)
            pltpu.make_async_remote_copy(
                send2.at[ch, t],
                recv2.at[ch, s],
                send_sem.at[1],
                r2.at[ch],
                device_id=(t, d),
                device_id_type=MESH,
            ).start()
            return inner

        lax.fori_loop(1, N_SLAB, post2, 0)
        recv2[ch, s] = send2[ch, s]
        return carry

    lax.fori_loop(0, CHUNKS, along_x, 0)
    loads[0].wait()
    loads[4].wait()
    three = pl.ds(0, N_DOM - 1)

    def deliver(n):
        target = ((s, left), (prv, d), (prv, left))[n - 1]
        parts[n] = jnp.broadcast_to(totals[n], (8, ATOMS))
        pltpu.make_async_remote_copy(
            parts.at[n], parts_in.at[n], send_sem.at[2 + n], r4.at[n], device_id=target, device_id_type=MESH
        ).start()

    def finish(ch, carry):
        @pl.when(ch < CHUNKS)
        def _():
            pltpu.make_async_copy(recv2.at[ch, others], recv2.at[ch, others], r2.at[ch]).wait()
            value = jnp.concatenate([recv2[ch, :, q].reshape(NY, C) for q in range(CHUNK)], 1)
            low, high = value[: NY // 2], value[NY // 2 :]
            even = dot3((even_m[0], even_m[1]), stacked(low + high, -1.0))
            odd = dot3((back_odd[0], back_odd[1]), stacked(low - high, -1.0))
            for q in range(CHUNK):
                lanes = slice(C * q, C * (q + 1))
                for e in range(N_DOM):
                    send3[ch, e, q, pl.ds(0, half, stride=2), :] = even[e * half : (e + 1) * half, lanes]
                    send3[ch, e, q, pl.ds(1, half, stride=2), :] = odd[e * half : (e + 1) * half, lanes]
            for i in range(1, N_DOM):
                e = (d + i) % N_DOM
                pltpu.make_async_remote_copy(
                    send3.at[ch, e],
                    recv3.at[ch, d],
                    send_sem.at[2],
                    r3.at[ch],
                    device_id=(s, e),
                    device_id_type=MESH,
                ).start()
            recv3[ch, d] = send3[ch, d]

        @pl.when(ch > 0)
        def _():
            c = ch - 1
            pltpu.make_async_copy(recv3.at[c, three], recv3.at[c, three], r3.at[c]).wait()
            columns = jnp.concatenate([recv3[c, e].reshape(CHUNK * ROWS, C) for e in range(N_DOM)], 1)
            block = dot3(split(columns), (fz[0], fz[1]))
            for q in range(CHUNK):
                pot_ref[CHUNK * c + q] = block[q * ROWS : (q + 1) * ROWS]
            done = pl.ds(pl.multiple_of(CHUNK * c, CHUNK), CHUNK)
            pltpu.make_async_copy(pot_ref.at[done], pot_hbm.at[done], pot_sem).start()
            both = split(block)
            edge = split(jnp.concatenate([block[q * ROWS : q * ROWS + 8] for q in range(CHUNK)], 0))

            def sample(g):
                u = dot3(both, (hot_z[g, 0], hot_z[g, 1]))
                v = dot3(edge, (hot_z[2 + g, 0], hot_z[2 + g, 1]))
                for q in range(CHUNK):
                    p = CHUNK * c + q
                    here = jnp.sum(u[q * ROWS : (q + 1) * ROWS] * wy_tab[g, :ROWS], 0, keepdims=True)
                    there = jnp.sum(v[q * 8 : (q + 1) * 8] * wy_tab[g, ROWS:], 0, keepdims=True)
                    totals[2 * g] += here * wx_tab[g, pl.ds(p, 1)]
                    totals[2 * g + 1] += there * wx_tab[2 + g, pl.ds(p, 1)]

            sample(0)

            @pl.when(c < CHUNKS - 1)
            def _():
                sample(1)

            @pl.when(c == CHUNKS - 2)
            def _():
                deliver(2)
                deliver(3)

        return carry

    lax.fori_loop(0, CHUNKS + 1, finish, 0)

    deliver(1)
    for n in range(1, 4):
        pltpu.make_async_copy(parts_in.at[n], parts_in.at[n], r4.at[n]).wait()
    total = totals[0] + parts_in[1, 0:1] + parts_in[2, 0:1] + parts_in[3, 0:1]
    grad_ref[...] = jnp.where(alive, total * (1.0 / (NX * NY * NZ)), 0.0)
    pltpu.make_async_copy(pot_ref, pot_hbm, pot_sem).wait()

    gone = atoms_ref.reshape(4 * N_DOM, 8, ATOMS).at[pl.ds(0, 4 * N_DOM - 1)]
    pltpu.make_async_copy(gone, gone, atom_send).wait()
    pltpu.make_async_copy(recv1.at[sent1], recv1.at[sent1], send_sem.at[0]).wait()

    def drain(ch, carry):
        pltpu.make_async_copy(send2.at[ch, others], send2.at[ch, others], send_sem.at[1]).wait()
        pltpu.make_async_copy(send3.at[ch, three], send3.at[ch, three], send_sem.at[2]).wait()
        return carry

    lax.fori_loop(0, CHUNKS, drain, 0)
    for n in range(1, 4):
        pltpu.make_async_copy(parts.at[n], parts.at[n], send_sem.at[2 + n]).wait()


def per_device(base_cells, offsets, charges, bias_coupling, counts, green):
    vmem = pl.BlockSpec(memory_space=pltpu.VMEM)
    hbm = pl.BlockSpec(memory_space=pltpu.HBM)
    potential, gradient = pl.pallas_call(
        main_kernel,
        out_shape=(
            jax.ShapeDtypeStruct((XD, ROWS, NZ), F32),
            jax.ShapeDtypeStruct((1, ATOMS), F32),
        ),
        in_specs=[vmem] * 4 + [hbm] * 2,
        out_specs=(hbm, vmem),
        scratch_shapes=[
            pltpu.VMEM((KY, C // 2, NX), F32),
            pltpu.VMEM((2, NZ, NZ), BF16),
            pltpu.VMEM((2, NX, 2 * NX), BF16),
            pltpu.VMEM((2, NX, 2 * NX), BF16),
            pltpu.VMEM((2, NX, 2 * NX), BF16),
            pltpu.VMEM((C, 256), BF16),
            pltpu.VMEM((8, ATOMS), F32),
            pltpu.VMEM((2, 2, N_DOM, 8, ATOMS), F32),
            pltpu.VMEM((KY, NX, C), F32),
            pltpu.VMEM((2, NX, 2 * NX), BF16),
            pltpu.VMEM((4, 2, NZ, ATOMS), BF16),
            pltpu.VMEM((2, ROWS + 8, ATOMS), F32),
            pltpu.VMEM((4, 8, ATOMS), F32),
            pltpu.VMEM((2, NY // 2, XD * C), F32),
            pltpu.VMEM((2, NY // 2, XD * C), F32),
            pltpu.VMEM((FAR, 2, XD, KY, C), F32),
            pltpu.VMEM((N_SLAB, XD, KY, C), F32),
            pltpu.VMEM((2, 2 * NX, KY * C), BF16),
            pltpu.VMEM((CHUNKS, N_SLAB, CHUNK, KY, C), F32),
            pltpu.VMEM((CHUNKS, N_SLAB, CHUNK, KY, C), F32),
            pltpu.VMEM((CHUNKS, N_DOM, CHUNK, ROWS, C), F32),
            pltpu.VMEM((CHUNKS, N_DOM, CHUNK, ROWS, C), F32),
            pltpu.VMEM((XD, ROWS, NZ), F32),
            pltpu.VMEM((4, 1, ATOMS), F32),
            pltpu.VMEM((4, 8, ATOMS), F32),
            pltpu.VMEM((4, 8, ATOMS), F32),
            pltpu.SemaphoreType.DMA((6,)),
            pltpu.SemaphoreType.DMA,
            pltpu.SemaphoreType.DMA((6,)),
            pltpu.SemaphoreType.DMA,
            pltpu.SemaphoreType.DMA((2, 2, N_DOM)),
            pltpu.SemaphoreType.DMA,
            pltpu.SemaphoreType.DMA((CHUNKS,)),
            pltpu.SemaphoreType.DMA((CHUNKS,)),
            pltpu.SemaphoreType.DMA((4,)),
        ],
        compiler_params=pltpu.CompilerParams(
            collective_id=1, has_side_effects=True, vmem_limit_bytes=64_500_000
        ),
        name="mesh",
    )(
        counts.reshape(1, 1),
        base_cells,
        offsets,
        charges.reshape(1, ATOMS),
        green.transpose(1, 2, 0),
        jnp.asarray(constants()),
    )
    norm = 1.0 / (NX * NY * NZ)
    gradient = bias_coupling * gradient.reshape(ATOMS)
    return (potential * norm, gradient)


def solution(mesh):
    placed = (
        P(None, ("slab", "dom")),
        P(None, ("slab", "dom")),
        P(("slab", "dom")),
        P(("slab", "dom")),
        P(("slab", "dom")),
        P(None, "slab", "dom"),
    )
    return jax.shard_map(
        per_device,
        mesh=mesh,
        in_specs=placed,
        out_specs=(P("slab", "dom", None), P(("slab", "dom"))),
        check_vma=False,
    )
```
